512 devices in a mesh: dp: 4 (over y), expert: 128 (over x, z, core).
Axes of the slice: x: 4, y: 4, z: 16, core: 2. Of those that a mesh axis runs over, the one named last changes fastest.
Arguments:
- tokens: bfloat16 [1024, 4096], P('expert', 'dp'), may hold values from -6 to 6
- output_gradient: bfloat16 [1024, 4096], P('expert', 'dp'), may hold values from -6 to 6
- routes: int32 [1024, 8], P('expert'), may hold values from 0 to 63, all different within a row; in each aligned block of 8 rows (0 to 7, 8 to 15, ...) at most 2 rows name the same one
- router_expert_weight: bfloat16 [1024, 8], P('expert'), may hold values from 0.049804688 to 0.5
- tenant: int32 [1024], P('expert'), may hold values from 0 to 3
- gate_weight: bfloat16 [128, 4096, 512], P('expert', 'dp'), may hold values from -0.09375 to 0.09375
- up_weight: bfloat16 [128, 4096, 512], P('expert', 'dp'), may hold values from -0.09375 to 0.09375
- down_weight: bfloat16 [128, 512, 4096], P('expert', None, 'dp'), may hold values from -0.09375 to 0.09375
- adapter_input_maps: bfloat16 [128, 4096, 2, 4, 8], P('expert', 'dp'), may hold values from -0.09375 to 0.09375
- adapter_output_maps: bfloat16 [128, 2, 4, 16, 512], P('expert'), may hold values from -0.359375 to 0.359375
Outputs:
- input_grad: bfloat16 [1024, 4096], P('expert', 'dp')
- adapter_a_grad: float32 [128, 4096, 2, 4, 8], P('expert', 'dp')
- adapter_b_grad: float32 [128, 2, 4, 16, 512], P('expert')
The draws below stay inside these ranges and needn't reach their ends.
Inputs may be any that keep to these rules, and one draw needn't show every extreme that they name: `routes`: among the 8 tokens of each aligned block of rows (the tokens of one index of the expert axis), no expert is chosen more than 2 times, a bound that some block reaches; a token's choices are distinct.
All inputs are finite; a program needn't handle non-finite values.
Results may differ from the reference program's by a relative error of at most 0.0065.
Values may be sent and summed in bfloat16 or wider, within the bound.
A program may use at most 64 MiB of HBM per device.

```python
import math
import jax
import jax.numpy as jnp
import numpy as np
from jax import lax

MODEL_WIDTH = 4096
EXPERT_HIDDEN = 1024
ADAPTER_RANK = 16
TENANT_COUNT = 4
TOK_COL = 8
ROUTED_EXPERTS = 64
TOPK = 8
CAP = 2
TOKENS = 1024
N_EXPERT = 128


def touch_ends(result, key, least, largest):
    index_at = [jax.random.randint(jax.random.fold_in(key, axis), (), 0, length) for axis, length in enumerate(result.shape)]
    widest = result.shape.index(max(result.shape))
    next_to = index_at[:widest] + [(index_at[widest] + 1) % result.shape[widest]] + index_at[widest + 1:]
    return result.at[tuple(index_at)].set(least).at[tuple(next_to)].set(largest)


def steps_of(stream_key, dims, cuts, low, high):
    def one(axis_at, parts):
        steps = jax.random.uniform(jax.random.fold_in(jax.random.fold_in(stream_key, 6), axis_at), (parts,), jnp.float32, low / len(cuts), high / len(cuts))
        return jnp.repeat(jnp.exp(steps), dims[axis_at] // parts).reshape((-1,) + (1,) * (len(dims) - axis_at - 1))

    level = one(*cuts[0])
    for cut in cuts[1:]:
        level = level * one(*cut)
    return level


def deal_out(key, own, number, rows, number_of, top, reach, slope):
    sequence = jax.random.permutation(key, number_of)
    heavy_load, common = portions_of(number_of, rows * top, reach, slope, True), portions_of(number_of, rows * top, reach, slope, False)
    places = jnp.arange(number_of)

    def named(lengths, offset_by):
        used = int((lengths > 0).sum())
        fixed = max(1, used // 4)
        shifted = fixed + (places - fixed + offset_by * (used - fixed)) % max(1, number_of - fixed)
        return jnp.zeros((number_of,), jnp.int32).at[sequence[jnp.where(places < fixed, places, shifted)]].set(jnp.asarray(lengths, jnp.int32))

    lengths = jnp.where(number % 4 == 0, named(heavy_load, number // 4), named(common, number - number // 4 - 1))
    mixed = jax.random.permutation(jax.random.fold_in(own, 3), number_of)
    giver, taker = mixed[0:number_of // 2 * 2:2], mixed[1:number_of // 2 * 2:2]
    margin = jnp.minimum(lengths[giver] - 1, reach - lengths[taker]) // 2
    margin = jnp.where((giver == sequence[0]) | (taker == sequence[0]) | (lengths[taker] == 0), 0, jnp.maximum(margin, 0))
    shifted = jax.random.randint(jax.random.fold_in(own, 4), (number_of // 2,), 0, 1 << 20) % (margin + 1)
    lengths = lengths.at[giver].add(-shifted).at[taker].add(shifted)
    items = jnp.searchsorted(jnp.cumsum(lengths), jnp.arange(rows * top), side="right").astype(jnp.int32)
    listing = items.reshape(top, rows).T
    listing = listing[jax.random.permutation(jax.random.fold_in(own, 1), rows)]
    offset_by = jax.random.randint(jax.random.fold_in(own, 2), (rows, 1), 0, top)
    return jnp.take_along_axis(listing, (jnp.arange(top)[None, :] + offset_by) % top, axis=1)


def portions_of(amount, total, most, skew, full):
    portions = [(1 << 20) // math.isqrt(grade ** skew) + 1 for grade in range(1, amount + 1)]
    largest = most if full else min(most, max(-(-total // amount), total * portions[0] // sum(portions)))
    least = 1 if total - largest >= amount - 1 else 0
    holding, rest = [largest] + [least] * (amount - 1), total - largest - least * (amount - 1)
    while rest > 0:
        free = [i for i in range(1, amount) if holding[i] < largest] or [i for i in range(1, amount) if holding[i] < most]
        whole, left = sum([portions[i] for i in free]), rest
        for i in free:
            more = min(most - holding[i], max(1, left * portions[i] // whole), rest)
            holding[i] = holding[i] + more
            rest = rest - more
    return np.array(holding)


def centred(own_key, dims, scale, bound, split=(), kind=jnp.bfloat16):
    entries = jax.random.normal(own_key, dims, jnp.float32) * scale
    if len(split) > 0:
        entries = steps_of(own_key, dims, split, -0.22, 0.18) * entries
    return jnp.clip(entries, min=-bound, max=bound).astype(kind)


def setup_inputs(seed: int = 0) -> dict:
    keys = jax.random.split(jax.random.key(seed), 11)
    tokens = centred(keys[0], (TOKENS, MODEL_WIDTH), 1.0, 6.0, ((0, 128), (1, 4)))
    output_gradient = centred(keys[1], (TOKENS, MODEL_WIDTH), 1.0, 6.0, ((0, 128), (1, 4)))
    routes_keys = jax.random.split(jax.random.fold_in(keys[2], 1), TOKENS // TOK_COL)
    routes_turns = jax.random.permutation(jax.random.fold_in(keys[2], 3), TOKENS // TOK_COL)
    routes = jax.vmap(lambda own, number: deal_out(jax.random.fold_in(keys[2], 2), own, number, TOK_COL, ROUTED_EXPERTS, TOPK, CAP, 2))(routes_keys, routes_turns).reshape((TOKENS, TOPK))
    router_expert_weight = jnp.clip(0.049804688 + 0.4501953 * jax.random.uniform(keys[3], (TOKENS, TOPK), jnp.float32) ** steps_of(keys[3], (TOKENS, TOPK), ((0, 128),), -0.2, 0.2), 0.049804688, 0.5).astype(jnp.bfloat16)
    tenant = touch_ends(jax.random.randint(keys[4], (TOKENS,), 0, TENANT_COUNT), jax.random.fold_in(keys[4], 1), 0, TENANT_COUNT - 1).astype(jnp.int32)
    gate_weight = centred(keys[5], (N_EXPERT, MODEL_WIDTH, EXPERT_HIDDEN // 2), MODEL_WIDTH ** -0.5, 0.09375, ((0, 128), (1, 4)))
    up_weight = centred(keys[6], (N_EXPERT, MODEL_WIDTH, EXPERT_HIDDEN // 2), MODEL_WIDTH ** -0.5, 0.09375, ((0, 128), (1, 4)))
    down_weight = centred(keys[7], (N_EXPERT, EXPERT_HIDDEN // 2, MODEL_WIDTH), MODEL_WIDTH ** -0.5, 0.09375, ((0, 128), (2, 4)))
    adapter_input_maps = centred(keys[8], (N_EXPERT, MODEL_WIDTH, 2, TENANT_COUNT, ADAPTER_RANK // 2), MODEL_WIDTH ** -0.5, 0.09375, ((0, 128), (1, 4)))
    adapter_output_maps = centred(keys[9], (N_EXPERT, 2, TENANT_COUNT, ADAPTER_RANK, EXPERT_HIDDEN // 2), 0.06, 0.359375, ((0, 128),))
    return dict(tokens=tokens, output_gradient=output_gradient, routes=routes, router_expert_weight=router_expert_weight, tenant=tenant, gate_weight=gate_weight, up_weight=up_weight, down_weight=down_weight, adapter_input_maps=adapter_input_maps, adapter_output_maps=adapter_output_maps)


ADAPTER_SCALE = 2.0


def product_leading(left, right):
    return lax.dot_general(left, right, (((0,), (0,)), ((), ())), preferred_element_type=jnp.float32)


def product_trailing(left, right):
    return lax.dot_general(left, right, (((1,), (1,)), ((), ())), preferred_element_type=jnp.float32)


def spread(values, tenant_mask):
    count = values.shape[0]
    wide = tenant_mask[:, None, :, None] * values.astype(jnp.float32).reshape(count, 2, 1, ADAPTER_RANK)
    return wide.reshape(count, 2, TENANT_COUNT * ADAPTER_RANK).astype(jnp.bfloat16)


def reference(tokens, output_gradient, routes, router_expert_weight, tenant, gate_weight, up_weight, down_weight, adapter_input_maps, adapter_output_maps):
    assigns = TOK_COL * TOPK
    flat_route = routes.reshape(N_EXPERT, assigns).astype(jnp.int32)
    expert_hot = (flat_route[:, :, None] == jnp.arange(ROUTED_EXPERTS, dtype=jnp.int32)[None, None, :]).astype(jnp.int32)
    earlier = jnp.cumsum(expert_hot, axis=1) - expert_hot
    position = jnp.sum(earlier * expert_hot, axis=2).astype(jnp.int32)
    column = jnp.broadcast_to(jnp.arange(N_EXPERT, dtype=jnp.int32)[:, None], (N_EXPERT, assigns))
    token_ids = (column * TOK_COL + (jnp.arange(assigns, dtype=jnp.int32) // TOPK)[None, :]).astype(jnp.int32)
    prob_flat = router_expert_weight.astype(jnp.float32).reshape(N_EXPERT, assigns)
    tenant_flat = tenant[token_ids]
    slot_token = jnp.full((ROUTED_EXPERTS, N_EXPERT, CAP), TOKENS, jnp.int32).at[flat_route, column, position].set(token_ids)
    slot_prob = jnp.zeros((ROUTED_EXPERTS, N_EXPERT, CAP), jnp.float32).at[flat_route, column, position].set(prob_flat)
    slot_tenant = jnp.full((ROUTED_EXPERTS, N_EXPERT, CAP), TENANT_COUNT, jnp.int32).at[flat_route, column, position].set(tenant_flat)
    padded_x = jnp.concatenate([tokens, jnp.zeros((1, MODEL_WIDTH), tokens.dtype)], axis=0)
    padded_dy = jnp.concatenate([output_gradient, jnp.zeros((1, MODEL_WIDTH), output_gradient.dtype)], axis=0)
    hidden_halfway = EXPERT_HIDDEN // 2
    rank_halfway = ADAPTER_RANK // 2

    def one_expert(operands):
        slot_ids, probs, tenants_of, gate_halves, up_halves, down_halves, a_halves, b_halves = operands
        gate_matrix = jnp.concatenate([gate_halves[0], gate_halves[1]], axis=1)
        up_matrix = jnp.concatenate([up_halves[0], up_halves[1]], axis=1)
        weight_down = jnp.concatenate([down_halves[0], down_halves[1]], axis=0)
        adapter_cols = jnp.concatenate([a_halves[0], a_halves[1]], axis=-1).reshape(MODEL_WIDTH, 2 * TENANT_COUNT * ADAPTER_RANK)
        adapter_b = jnp.concatenate([b_halves[0], b_halves[1]], axis=-1)
        gate_output_map = adapter_b[0].reshape(TENANT_COUNT * ADAPTER_RANK, EXPERT_HIDDEN)
        up_output_map = adapter_b[1].reshape(TENANT_COUNT * ADAPTER_RANK, EXPERT_HIDDEN)
        input_rows = padded_x[slot_ids]
        rows_dy = padded_dy[slot_ids]
        count = slot_ids.shape[0]
        tenant_mask = (tenants_of[:, None] == jnp.arange(TENANT_COUNT, dtype=jnp.int32)[None, :]).astype(jnp.float32)
        proj_all = jnp.dot(input_rows, adapter_cols, preferred_element_type=jnp.float32).reshape(count, 2, TENANT_COUNT, ADAPTER_RANK)
        proj_low = jnp.sum(proj_all * tenant_mask[:, None, :, None], axis=2).astype(jnp.bfloat16)
        projection_spread = spread(proj_low, tenant_mask)
        gate_preactivation = jnp.dot(input_rows, gate_matrix, preferred_element_type=jnp.float32) + ADAPTER_SCALE * jnp.dot(projection_spread[:, 0], gate_output_map, preferred_element_type=jnp.float32)
        up_preactivation = jnp.dot(input_rows, up_matrix, preferred_element_type=jnp.float32) + ADAPTER_SCALE * jnp.dot(projection_spread[:, 1], up_output_map, preferred_element_type=jnp.float32)
        act_grad = probs[:, None] * product_trailing(rows_dy, weight_down)
        gate_sig = jax.nn.sigmoid(gate_preactivation)
        gate_gradient = (act_grad * up_preactivation * gate_sig * (1.0 + gate_preactivation * (1.0 - gate_sig))).astype(jnp.bfloat16)
        up_gradient = (act_grad * gate_preactivation * gate_sig).astype(jnp.bfloat16)
        output_map_gradient = ADAPTER_SCALE * jnp.stack([product_leading(projection_spread[:, 0], gate_gradient), product_leading(projection_spread[:, 1], up_gradient)])
        backward_total = ADAPTER_SCALE * jnp.stack([product_trailing(gate_gradient, gate_output_map), product_trailing(up_gradient, up_output_map)], axis=1)
        back_low = jnp.sum(backward_total.reshape(count, 2, TENANT_COUNT, ADAPTER_RANK) * tenant_mask[:, None, :, None], axis=2).astype(jnp.bfloat16)
        back_spread = spread(back_low, tenant_mask).reshape(count, 2 * TENANT_COUNT * ADAPTER_RANK)
        grad_a = product_leading(input_rows, back_spread).reshape(MODEL_WIDTH, 2, TENANT_COUNT, ADAPTER_RANK)
        slot_grad = (product_trailing(gate_gradient, gate_matrix) + product_trailing(up_gradient, up_matrix) + product_trailing(back_spread, adapter_cols)).astype(jnp.bfloat16)
        return slot_grad, grad_a, output_map_gradient.reshape(2, TENANT_COUNT, ADAPTER_RANK, EXPERT_HIDDEN)

    operands = (
        slot_token.reshape(ROUTED_EXPERTS, N_EXPERT * CAP),
        slot_prob.reshape(ROUTED_EXPERTS, N_EXPERT * CAP),
        slot_tenant.reshape(ROUTED_EXPERTS, N_EXPERT * CAP),
        gate_weight.reshape(ROUTED_EXPERTS, 2, MODEL_WIDTH, hidden_halfway),
        up_weight.reshape(ROUTED_EXPERTS, 2, MODEL_WIDTH, hidden_halfway),
        down_weight.reshape(ROUTED_EXPERTS, 2, hidden_halfway, MODEL_WIDTH),
        adapter_input_maps.reshape(ROUTED_EXPERTS, 2, MODEL_WIDTH, 2, TENANT_COUNT, rank_halfway),
        adapter_output_maps.reshape(ROUTED_EXPERTS, 2, 2, TENANT_COUNT, ADAPTER_RANK, hidden_halfway),
    )
    slot_grads, grads_a, grads_b = lax.map(one_expert, operands)
    total = jnp.zeros((TOKENS + 1, MODEL_WIDTH), jnp.float32).at[slot_token.reshape(-1)].add(slot_grads.reshape(-1, MODEL_WIDTH).astype(jnp.float32))
    input_grad = total[:TOKENS].astype(jnp.bfloat16)
    adapter_a_grad = grads_a.reshape(ROUTED_EXPERTS, MODEL_WIDTH, 2, TENANT_COUNT, 2, rank_halfway).transpose(0, 4, 1, 2, 3, 5).reshape(N_EXPERT, MODEL_WIDTH, 2, TENANT_COUNT, rank_halfway)
    adapter_b_grad = grads_b.reshape(ROUTED_EXPERTS, 2, TENANT_COUNT, ADAPTER_RANK, 2, hidden_halfway).transpose(0, 4, 1, 2, 3, 5).reshape(N_EXPERT, 2, TENANT_COUNT, ADAPTER_RANK, hidden_halfway)
    return input_grad, adapter_a_grad, adapter_b_grad
```

```python
import functools

import jax
import jax.numpy as jnp
from jax import lax
from jax.experimental import pallas as pl
from jax.experimental.pallas import tpu as pltpu
from jax.sharding import PartitionSpec as P

ADAPTER_SCALE = 2.0
CHIPS_X = 4
BF = jnp.bfloat16
F32 = jnp.float32
MESH = pl.DeviceIdType.MESH


def mm(a, b):
    return lax.dot_general(a, b, (((1,), (0,)), ((), ())), preferred_element_type=F32)


def mm_t(a, b):
    return lax.dot_general(a, b, (((1,), (1,)), ((), ())), preferred_element_type=F32)


def iota(shape, axis):
    return lax.broadcasted_iota(jnp.int32, shape, axis)


def kernel(
    nx,
    nz,
    ny,
    tok,
    dy,
    routes,
    prob,
    ten,
    a_own,
    b_map,
    wg_hbm,
    wu_hbm,
    wd_hbm,
    ig_out,
    ag_out,
    bg_out,
    wg,
    wu,
    wd,
    pg,
    sel,
    rs,
    rr,
    afull,
    part_f,
    part_b,
    proj_f,
    proj_b,
    yr,
    yx,
    dgu,
    xsf,
    qs,
    qr,
    rsend,
    rrecv,
    sb,
    xb,
    tz,
    fb,
    w_sem,
    a_sem,
    ring_s,
    ring_r,
    xs_sem,
    xr_sem,
    cs_sem,
    cr_sem,
    ys_sem,
    yr_sem,
    gs_sem,
    gr_sem,
    q_sem,
    rc_s,
    rc_r,
    bx_s,
    bx_r,
    bz_s,
    bz_r,
):
    me = lax.axis_index("expert")
    y = lax.axis_index("dp")
    c = lax.rem(me, 2)
    z = lax.rem(lax.div(me, 2), nz)
    x = lax.div(me, 2 * nz)
    width = tok.shape[1]
    hid = wg.shape[1]
    ntok = tok.shape[0]
    lm = 2 * nx * nz
    pw = 2 * width + lm + 128
    sw = 2 * width + 128
    slots_x = 2 * nz
    half = pw // 2

    def eid(xx, zz, cc):
        return (xx * nz + zz) * 2 + cc

    partner = eid(x, z, 1 - c)
    zr = eid(x, lax.rem(z + 1, nz), c)
    zl = eid(x, lax.rem(z + nz - 1, nz), c)

    def rcopy(src, dst, s_sem, r_sem, dev):
        return pltpu.make_async_remote_copy(
            src_ref=src,
            dst_ref=dst,
            send_sem=s_sem,
            recv_sem=r_sem,
            device_id={"expert": dev},
            device_id_type=MESH,
        )

    def ycopy(src, dst, s_sem, r_sem, dev):
        return pltpu.make_async_remote_copy(
            src_ref=src,
            dst_ref=dst,
            send_sem=s_sem,
            recv_sem=r_sem,
            device_id={"dp": dev},
            device_id_type=MESH,
        )

    barrier = pltpu.get_barrier_semaphore()
    x_others = [lax.rem(x + d, nx) for d in ((2, 1, 3) if nx == 4 else range(1, nx))]
    y_others = [lax.rem(y + d, ny) for d in ((2, 1, 3) if ny == 4 else range(1, ny))]
    near = [zr, zl, partner] + [eid(o, z, c) for o in x_others]
    for dev in near:
        pl.semaphore_signal(barrier, inc=1, device_id={"expert": dev}, device_id_type=MESH)
    for dev in y_others:
        pl.semaphore_signal(barrier, inc=1, device_id={"dp": dev}, device_id_type=MESH)

    w_copies = [
        pltpu.make_async_copy(wg_hbm, wg, w_sem.at[0]),
        pltpu.make_async_copy(wu_hbm, wu, w_sem.at[1]),
        pltpu.make_async_copy(wd_hbm, wd, w_sem.at[2]),
    ]
    for w_copy in w_copies:
        w_copy.start()

    col = iota((ntok, lm), 1)
    row = iota((ntok, lm), 0)
    col_expert = lax.div(lax.rem(col, 2 * nx), 2) * nz + lax.div(col, 2 * nx)
    col_pos = lax.rem(col, 2)
    hit = jnp.zeros((ntok, lm), jnp.int32)
    weight = jnp.zeros((ntok, lm), F32)
    chosen = routes[...]
    probs = prob[...].astype(F32)
    for k in range(routes.shape[1]):
        same = chosen[:, k : k + 1] == col_expert
        hit = hit + same.astype(jnp.int32)
        weight = weight + jnp.where(same, probs[:, k : k + 1], 0.0)
    before = jnp.zeros((ntok, lm), jnp.int32)
    for n in range(ntok - 1):
        before = before + jnp.where(row > n, hit[n : n + 1, :], 0)
    weight = jnp.where(before == col_pos, weight, 0.0)
    lane_ten = lax.rem(lax.div(iota((ntok, 128), 1), 16), 4)
    ten_hot = (ten[...] == lane_ten).astype(F32)
    pg[z, :, 0:width] = tok[...]
    pg[z, :, width : 2 * width] = dy[...]
    pg[z, :, 2 * width : 2 * width + lm] = weight.astype(BF)
    pg[z, :, 2 * width + lm : pw] = ten_hot.astype(BF)
    afull[:, c] = a_own[...]

    pl.semaphore_wait(barrier, len(near) + len(y_others))

    a_copy = rcopy(a_own, afull.at[:, c], a_sem.at[0], a_sem.at[1], partner)

    far = nz // 2

    def ring(direction, step, piece):
        cols = pl.ds(piece * half, half)
        if direction == 0:
            block = lax.rem(z - step + 1 + nz, nz)
            dev = zr
        else:
            block = lax.rem(z + step - 1, nz)
            dev = zl
        ref = pg.at[block, :, cols]
        at = (direction * far + step - 1) * 2 + piece
        return rcopy(ref, ref, ring_s.at[at], ring_r.at[at], dev)

    sends = []
    for step in range(1, far + 1):
        for piece in range(2):
            for direction in range(2):
                if direction == 1 and step == far:
                    continue
                if step > 1:
                    ring(direction, step - 1, piece).wait_recv()
                copy = ring(direction, step, piece)
                copy.start()
                sends.append(copy)
        if step == 1:
            a_copy.start()
            sends.append(a_copy)
    for piece in range(2):
        ring(0, far, piece).wait_recv()
        if far > 1:
            ring(1, far - 1, piece).wait_recv()

    count = nz * ntok
    slots = nx * slots_x
    gathered = pg[...].astype(F32).reshape(count, pw).astype(BF)
    meta = gathered[:, 2 * width : 2 * width + lm]
    tenants = gathered[:, 2 * width + lm : pw]
    j = iota((slots, lm), 0)
    pick = (
        iota((slots, lm), 1) == z * (2 * nx) + lax.div(j, slots_x) * 2 + lax.rem(j, 2)
    ).astype(BF)
    slot_z = lax.div(lax.rem(iota((slots, count), 0), slots_x), 2)
    tok_z = lax.div(iota((slots, count), 1), ntok)
    weights_t = jnp.where(slot_z == tok_z, mm_t(pick, meta), 0.0)
    select_t = (weights_t > 0).astype(BF)
    slot_z2 = lax.div(lax.rem(iota((count, slots), 1), slots_x), 2)
    tok_z2 = lax.div(iota((count, slots), 0), ntok)
    weights_n = jnp.where(slot_z2 == tok_z2, mm_t(meta, pick), 0.0)
    sel[...] = (weights_n > 0).astype(BF)
    rs[:, :, 0 : 2 * width] = (
        mm(select_t, gathered[:, 0 : 2 * width]).astype(BF).reshape(nx, slots_x, 2 * width)
    )
    rs[:, :, 2 * width : sw] = (
        mm(weights_t.astype(BF), tenants).astype(BF).reshape(nx, slots_x, 128)
    )

    for i, o in enumerate(x_others):
        copy = rcopy(rs.at[o], rr.at[c, x], xs_sem.at[i], xr_sem.at[i], eid(o, z, c))
        copy.start()
        sends.append(copy)
    copy = rcopy(rs.at[x], rr.at[c, x], cs_sem.at[nx - 1], cr_sem.at[nx - 1], partner)
    copy.start()
    sends.append(copy)
    rr[c, x] = rs[x]
    back = (2, 3, 1) if nx == 4 else range(nx - 1, 0, -1)
    x_from = [lax.rem(x + d, nx) for d in back]
    for i, o in enumerate(x_from):
        block = rr.at[c, o]
        rcopy(block, block, xs_sem.at[i], xr_sem.at[i], eid(o, z, c)).wait_recv()
        copy = rcopy(block, block, cs_sem.at[i], cr_sem.at[i], partner)
        copy.start()
        sends.append(copy)
    for i, o in enumerate(x_from + [x]):
        block = rr.at[1 - c, o]
        rcopy(block, block, cs_sem.at[i], cr_sem.at[i], partner).wait_recv()
    rcopy(a_own, afull.at[:, 1 - c], a_sem.at[0], a_sem.at[1], partner).wait_recv()

    rows = 2 * slots
    quarter = rows // ny
    tag = rr[:, :, :, 2 * width : sw].reshape(rows, 128).astype(F32)
    mask = tag > 0
    slot_prob = jnp.max(tag, axis=1, keepdims=True)
    xin = rr[:, :, :, 0:width].reshape(rows, width)
    dyin = rr[:, :, :, width : 2 * width].reshape(rows, width)
    at = afull[...].astype(F32).reshape(128, width).astype(BF)

    def y_send(index, src, dst):
        for i, o in enumerate(y_others):
            copy = ycopy(src(o), dst, ys_sem.at[index, i], yr_sem.at[index, i], o)
            copy.start()
            sends.append(copy)

    def put(index, value):
        part_f[index] = value
        part_b[index] = value.astype(BF).reshape(ny, quarter, hid)
        y_send(index, lambda o: part_b.at[index, o], yr.at[index, y])

    w_copies[0].wait()
    put(0, mm(xin, wg[...]))
    w_copies[1].wait()
    put(1, mm(xin, wu[...]))
    w_copies[2].wait()
    put(2, mm_t(dyin, wd[...]) * slot_prob)
    projected = jnp.where(mask, mm_t(xin, at), 0.0)
    proj_f[...] = projected
    proj_b[...] = projected.astype(BF).reshape(ny, quarter, 128)
    y_send(3, lambda o: proj_b.at[o], yx.at[y])

    y_back = (2, 3, 1) if ny == 4 else range(ny - 1, 0, -1)
    y_from = [lax.rem(y + d, ny) for d in y_back]
    mine = pl.ds(pl.multiple_of(y * quarter, quarter), quarter)

    def total(index):
        value = part_f[index, mine, :]
        for i, o in enumerate(y_from):
            block = yr.at[index, o]
            ycopy(block, block, ys_sem.at[index, i], yr_sem.at[index, i], o).wait_recv()
            value = value + yr[index, o].astype(F32)
        return value

    gate = total(0)
    up = total(1)
    act = total(2)
    low = proj_f[mine, :]
    for i, o in enumerate(y_from):
        block = yx.at[o]
        ycopy(block, block, ys_sem.at[3, i], yr_sem.at[3, i], o).wait_recv()
        low = low + yx[o].astype(F32)
    lane = iota((quarter, 128), 1)
    bmap = b_map[...]
    gate = gate + ADAPTER_SCALE * mm(jnp.where(lane < 64, low, 0.0).astype(BF), bmap)
    up = up + ADAPTER_SCALE * mm(jnp.where(lane < 64, 0.0, low).astype(BF), bmap)
    sig = 1.0 / (1.0 + jnp.exp(-gate))
    dgu[y, :, 0:hid] = (act * up * sig * (1.0 + gate * (1.0 - sig))).astype(BF)
    dgu[y, :, hid : 2 * hid] = (act * gate * sig).astype(BF)
    xsf[y] = low.astype(BF)
    for i, o in enumerate(y_others):
        copy = ycopy(dgu.at[y], dgu.at[y], gs_sem.at[0, i], gr_sem.at[0, i], o)
        copy.start()
        sends.append(copy)
    for i, o in enumerate(y_others):
        copy = ycopy(xsf.at[y], xsf.at[y], gs_sem.at[1, i], gr_sem.at[1, i], o)
        copy.start()
        sends.append(copy)
    for i, o in enumerate(y_from):
        block = dgu.at[o]
        ycopy(block, block, gs_sem.at[0, i], gr_sem.at[0, i], o).wait_recv()
    for i, o in enumerate(y_from):
        block = xsf.at[o]
        ycopy(block, block, gs_sem.at[1, i], gr_sem.at[1, i], o).wait_recv()

    hq = ny // 2
    wide = iota((slots, 128), 1)

    def back_half(which):
        group = pl.ds(which * hq, hq)
        dg = dgu[group, :, 0:hid].reshape(slots, hid)
        du = dgu[group, :, hid : 2 * hid].reshape(slots, hid)
        marks = rr[which, :, :, 2 * width : sw].reshape(slots, 128).astype(F32) > 0
        q = jnp.where(wide < 64, mm_t(dg, bmap), mm_t(du, bmap))
        q = jnp.where(marks, ADAPTER_SCALE * q, 0.0)
        r = mm_t(dg, wg[...]) + mm_t(du, wu[...]) + mm(q.astype(BF), at)
        qs[which] = q
        return r.reshape(nx, slots_x, width)

    rsend[...] = back_half(1 - c).astype(BF)
    order = x_others + [x]
    order_from = x_from + [x]
    for i, o in enumerate(order):
        copy = rcopy(rsend.at[o], rrecv.at[o], rc_s.at[i], rc_r.at[i], partner)
        copy.start()
        sends.append(copy)
    sb[...] = back_half(c).astype(BF)
    q_copy = rcopy(qs, qr, q_sem.at[0], q_sem.at[1], partner)
    q_copy.start()
    sends.append(q_copy)
    for i, o in enumerate(order):
        block = rrecv.at[o]
        rcopy(block, block, rc_s.at[i], rc_r.at[i], partner).wait_recv()
        both = (sb[o].astype(F32) + rrecv[o].astype(F32)).astype(BF)
        if i < nx - 1:
            sb[o] = both
            copy = rcopy(sb.at[o], xb.at[x], bx_s.at[i], bx_r.at[i], eid(o, z, c))
            copy.start()
            sends.append(copy)
        else:
            xb[o] = both

    dg = dgu[:, :, 0:hid].reshape(rows, hid)
    du = dgu[:, :, hid : 2 * hid].reshape(rows, hid)
    low_t = xsf[...].reshape(rows, 128).astype(F32).T.astype(BF)
    bg_rows = iota((128, hid), 0)
    bg_out[...] = ADAPTER_SCALE * jnp.where(bg_rows < 64, mm(low_t, dg), mm(low_t, du))

    for i, o in enumerate(x_from):
        block = xb.at[o]
        rcopy(block, block, bx_s.at[i], bx_r.at[i], eid(o, z, c)).wait_recv()
    by_token = mm(sel[...], xb[...].reshape(slots, width))
    tz[...] = by_token.reshape(nz, ntok, width).astype(BF)
    dist = []
    for d in range(far, 0, -1):
        dist.append(d)
        if d != nz - d:
            dist.append(nz - d)
    for i, d in enumerate(dist):
        o = lax.rem(z + d, nz)
        copy = rcopy(tz.at[o], fb.at[z], bz_s.at[d - 1], bz_r.at[d - 1], eid(x, o, c))
        copy.start()
        sends.append(copy)
    fb[z] = tz[z]

    q_copy.wait_recv()
    q_all = (qs[...] + qr[...]).reshape(rows, 128)
    ag = mm(q_all.T.astype(BF), xin).reshape(8, 2, 8, width)
    ag_out[...] = jnp.where(c == 0, ag[:, 0], ag[:, 1])

    for d in dist:
        o = lax.rem(z + nz - d, nz)
        block = fb.at[o]
        rcopy(block, block, bz_s.at[d - 1], bz_r.at[d - 1], eid(x, o, c)).wait_recv()
    ig_out[...] = jnp.sum(fb[...].astype(F32), axis=0).astype(BF)
    for copy in sends:
        copy.wait_send()


def shards(
    tokens,
    output_gradient,
    routes,
    router_expert_weight,
    tenant,
    gate_weight,
    up_weight,
    down_weight,
    adapter_input_maps,
    adapter_output_maps,
    nx=CHIPS_X,
):
    devices = lax.axis_size("expert")
    ny = lax.axis_size("dp")
    nz = devices // (2 * nx)
    ntok, width = tokens.shape
    hid = gate_weight.shape[2]
    slots_x = 2 * nz
    slots = nx * slots_x
    rows = 2 * slots
    quarter = rows // ny
    lm = slots
    pw = 2 * width + lm + 128
    sw = 2 * width + 128
    a_own = jnp.transpose(adapter_input_maps[0], (1, 2, 3, 0)).reshape(8, 8, width)
    b_map = adapter_output_maps.reshape(128, hid)
    vmem = pl.BlockSpec(memory_space=pltpu.VMEM)
    anywhere = pl.BlockSpec(memory_space=pl.ANY)
    dma = pltpu.SemaphoreType.DMA
    far = nz // 2
    ig, ag, bg = pl.pallas_call(
        functools.partial(kernel, nx, nz, ny),
        out_shape=(
            jax.ShapeDtypeStruct((ntok, width), BF),
            jax.ShapeDtypeStruct((8, 8, width), F32),
            jax.ShapeDtypeStruct((128, hid), F32),
        ),
        in_specs=[vmem] * 7 + [anywhere] * 3,
        out_specs=(vmem, vmem, vmem),
        scratch_shapes=[
            pltpu.VMEM((width, hid), BF),
            pltpu.VMEM((width, hid), BF),
            pltpu.VMEM((hid, width), BF),
            pltpu.VMEM((nz, ntok, pw), BF),
            pltpu.VMEM((nz * ntok, slots), BF),
            pltpu.VMEM((nx, slots_x, sw), BF),
            pltpu.VMEM((2, nx, slots_x, sw), BF),
            pltpu.VMEM((8, 2, 8, width), BF),
            pltpu.VMEM((3, rows, hid), F32),
            pltpu.VMEM((3, ny, quarter, hid), BF),
            pltpu.VMEM((rows, 128), F32),
            pltpu.VMEM((ny, quarter, 128), BF),
            pltpu.VMEM((3, ny, quarter, hid), BF),
            pltpu.VMEM((ny, quarter, 128), BF),
            pltpu.VMEM((ny, quarter, 2 * hid), BF),
            pltpu.VMEM((ny, quarter, 128), BF),
            pltpu.VMEM((2, slots, 128), F32),
            pltpu.VMEM((2, slots, 128), F32),
            pltpu.VMEM((nx, slots_x, width), BF),
            pltpu.VMEM((nx, slots_x, width), BF),
            pltpu.VMEM((nx, slots_x, width), BF),
            pltpu.VMEM((nx, slots_x, width), BF),
            pltpu.VMEM((nz, ntok, width), BF),
            pltpu.VMEM((nz, ntok, width), BF),
            dma((3,)),
            dma((2,)),
            dma((4 * far,)),
            dma((4 * far,)),
            dma((nx - 1,)),
            dma((nx - 1,)),
            dma((nx,)),
            dma((nx,)),
            dma((4, ny - 1)),
            dma((4, ny - 1)),
            dma((2, ny - 1)),
            dma((2, ny - 1)),
            dma((2,)),
            dma((nx,)),
            dma((nx,)),
            dma((nx - 1,)),
            dma((nx - 1,)),
            dma((nz - 1,)),
            dma((nz - 1,)),
        ],
        compiler_params=pltpu.CompilerParams(collective_id=0, has_side_effects=True),
        name="layer_backward",
    )(
        tokens,
        output_gradient,
        routes,
        router_expert_weight,
        tenant.reshape(ntok, 1),
        a_own,
        b_map,
        gate_weight[0],
        up_weight[0],
        down_weight[0],
    )
    adapter_a_grad = jnp.transpose(ag.reshape(2, 4, 8, width), (3, 0, 1, 2))[None]
    adapter_b_grad = bg.reshape(1, 2, 4, 16, hid)
    return (ig, adapter_a_grad, adapter_b_grad)


def solution(mesh):
    placed = (
        P("expert", "dp"),
        P("expert", "dp"),
        P("expert", None),
        P("expert", None),
        P("expert"),
        P("expert", "dp", None),
        P("expert", "dp", None),
        P("expert", None, "dp"),
        P("expert", "dp", None, None, None),
        P("expert", None, None, None, None),
    )
    return jax.shard_map(
        shards,
        mesh=mesh,
        in_specs=placed,
        out_specs=(
            P("expert", "dp"),
            P("expert", "dp", None, None, None),
            P("expert", None, None, None, None),
        ),
        check_vma=False,
    )
```

```python
import functools

import jax
import jax.numpy as jnp
from jax import lax
from jax.experimental import pallas as pl
from jax.experimental.pallas import tpu as pltpu
from jax.sharding import PartitionSpec as P

ADAPTER_SCALE = 2.0
CHIPS_X = 4
HOP = 2
BF = jnp.bfloat16
F32 = jnp.float32
MESH = pl.DeviceIdType.MESH


def mm(a, b):
    return lax.dot_general(a, b, (((1,), (0,)), ((), ())), preferred_element_type=F32)


def mm_t(a, b):
    return lax.dot_general(a, b, (((1,), (1,)), ((), ())), preferred_element_type=F32)


def iota(shape, axis):
    return lax.broadcasted_iota(jnp.int32, shape, axis)


def kernel(
    nx,
    nz,
    ny,
    tok,
    dy,
    routes,
    prob,
    ten,
    a_own,
    b_map,
    wg_hbm,
    wu_hbm,
    wd_hbm,
    ig_out,
    ag_out,
    bg_out,
    wg,
    wu,
    wd,
    pg,
    sel,
    rs,
    rr,
    afull,
    part_f,
    part_b,
    proj_f,
    proj_b,
    yr,
    yx,
    dgu,
    xsf,
    qs,
    qr,
    rsend,
    rrecv,
    sb,
    xb,
    tz,
    fb,
    w_sem,
    a_sem,
    ring_s,
    ring_r,
    xs_sem,
    xr_sem,
    cs_sem,
    cr_sem,
    ys_sem,
    yr_sem,
    gs_sem,
    gr_sem,
    q_sem,
    rc_s,
    rc_r,
    bx_s,
    bx_r,
    bz_s,
    bz_r,
):
    me = lax.axis_index("expert")
    y = lax.axis_index("dp")
    c = lax.rem(me, 2)
    z = lax.rem(lax.div(me, 2), nz)
    x = lax.div(me, 2 * nz)
    width = tok.shape[1]
    hid = wg.shape[1]
    ntok = tok.shape[0]
    lm = 2 * nx * nz
    pw = 2 * width + lm + 128
    sw = 2 * width + 128
    slots_x = 2 * nz

    def eid(xx, zz, cc):
        return (xx * nz + zz) * 2 + cc

    partner = eid(x, z, 1 - c)
    z_near = []
    for d in range(1, nz):
        z_near.append(eid(x, lax.rem(z + d, nz), c))

    def rcopy(src, dst, s_sem, r_sem, dev):
        return pltpu.make_async_remote_copy(
            src_ref=src,
            dst_ref=dst,
            send_sem=s_sem,
            recv_sem=r_sem,
            device_id={"expert": dev},
            device_id_type=MESH,
        )

    def ycopy(src, dst, s_sem, r_sem, dev):
        return pltpu.make_async_remote_copy(
            src_ref=src,
            dst_ref=dst,
            send_sem=s_sem,
            recv_sem=r_sem,
            device_id={"dp": dev},
            device_id_type=MESH,
        )

    barrier = pltpu.get_barrier_semaphore()
    x_others = [lax.rem(x + d, nx) for d in ((2, 1, 3) if nx == 4 else range(1, nx))]
    y_others = [lax.rem(y + d, ny) for d in ((2, 1, 3) if ny == 4 else range(1, ny))]
    near = z_near + [partner] + [eid(o, z, c) for o in x_others]
    for dev in near:
        pl.semaphore_signal(barrier, inc=1, device_id={"expert": dev}, device_id_type=MESH)
    for dev in y_others:
        pl.semaphore_signal(barrier, inc=1, device_id={"dp": dev}, device_id_type=MESH)

    w_copies = [
        pltpu.make_async_copy(wg_hbm, wg, w_sem.at[0]),
        pltpu.make_async_copy(wu_hbm, wu, w_sem.at[1]),
        pltpu.make_async_copy(wd_hbm, wd, w_sem.at[2]),
    ]
    for w_copy in w_copies:
        w_copy.start()

    col = iota((ntok, lm), 1)
    row = iota((ntok, lm), 0)
    col_expert = lax.div(lax.rem(col, 2 * nx), 2) * nz + lax.div(col, 2 * nx)
    col_pos = lax.rem(col, 2)
    hit = jnp.zeros((ntok, lm), jnp.int32)
    weight = jnp.zeros((ntok, lm), F32)
    chosen = routes[...]
    probs = prob[...].astype(F32)
    for k in range(routes.shape[1]):
        same = chosen[:, k : k + 1] == col_expert
        hit = hit + same.astype(jnp.int32)
        weight = weight + jnp.where(same, probs[:, k : k + 1], 0.0)
    before = jnp.zeros((ntok, lm), jnp.int32)
    for n in range(ntok - 1):
        before = before + jnp.where(row > n, hit[n : n + 1, :], 0)
    weight = jnp.where(before == col_pos, weight, 0.0)
    lane_ten = lax.rem(lax.div(iota((ntok, 128), 1), 16), 4)
    ten_hot = (ten[...] == lane_ten).astype(F32)
    pg[z, :, 0:width] = tok[...]
    pg[z, :, width : 2 * width] = dy[...]
    pg[z, :, 2 * width : 2 * width + lm] = weight.astype(BF)
    pg[z, :, 2 * width + lm : pw] = ten_hot.astype(BF)
    afull[:, c] = a_own[...]

    pl.semaphore_wait(barrier, len(near) + len(y_others))

    a_copy = rcopy(a_own, afull.at[:, c], a_sem.at[0], a_sem.at[1], partner)

    far = nz // 2

    def ring(direction, d):
        skip = min(d, HOP)
        have = d - skip
        if direction == 0:
            block = lax.rem(z - have + nz, nz)
            dev = lax.rem(z + skip, nz)
        else:
            block = lax.rem(z + have, nz)
            dev = lax.rem(z + nz - skip, nz)
        ref = pg.at[block]
        at = direction * far + d - 1
        return rcopy(ref, ref, ring_s.at[at], ring_r.at[at], eid(x, dev, c))

    sends = []
    for d in range(1, far + 1):
        for direction in range(2):
            if direction == 1 and d == far:
                continue
            if d > HOP:
                ring(direction, d - HOP).wait_recv()
            copy = ring(direction, d)
            copy.start()
            sends.append(copy)
        if d == min(HOP, far):
            a_copy.start()
            sends.append(a_copy)
    for direction in range(2):
        last = far - direction
        for d in range(max(1, last - HOP + 1), last + 1):
            ring(direction, d).wait_recv()

    count = nz * ntok
    slots = nx * slots_x
    gathered = pg[...].astype(F32).reshape(count, pw).astype(BF)
    meta = gathered[:, 2 * width : 2 * width + lm]
    tenants = gathered[:, 2 * width + lm : pw]
    j = iota((slots, lm), 0)
    pick = (
        iota((slots, lm), 1) == z * (2 * nx) + lax.div(j, slots_x) * 2 + lax.rem(j, 2)
    ).astype(BF)
    slot_z = lax.div(lax.rem(iota((slots, count), 0), slots_x), 2)
    tok_z = lax.div(iota((slots, count), 1), ntok)
    weights_t = jnp.where(slot_z == tok_z, mm_t(pick, meta), 0.0)
    select_t = (weights_t > 0).astype(BF)
    slot_z2 = lax.div(lax.rem(iota((count, slots), 1), slots_x), 2)
    tok_z2 = lax.div(iota((count, slots), 0), ntok)
    weights_n = jnp.where(slot_z2 == tok_z2, mm_t(meta, pick), 0.0)
    sel[...] = (weights_n > 0).astype(BF)
    rs[:, :, 0 : 2 * width] = (
        mm(select_t, gathered[:, 0 : 2 * width]).astype(BF).reshape(nx, slots_x, 2 * width)
    )
    rs[:, :, 2 * width : sw] = (
        mm(weights_t.astype(BF), tenants).astype(BF).reshape(nx, slots_x, 128)
    )

    for i, o in enumerate(x_others):
        copy = rcopy(rs.at[o], rr.at[c, x], xs_sem.at[i], xr_sem.at[i], eid(o, z, c))
        copy.start()
        sends.append(copy)
    copy = rcopy(rs.at[x], rr.at[c, x], cs_sem.at[nx - 1], cr_sem.at[nx - 1], partner)
    copy.start()
    sends.append(copy)
    rr[c, x] = rs[x]
    back = (2, 3, 1) if nx == 4 else range(nx - 1, 0, -1)
    x_from = [lax.rem(x + d, nx) for d in back]
    for i, o in enumerate(x_from):
        block = rr.at[c, o]
        rcopy(block, block, xs_sem.at[i], xr_sem.at[i], eid(o, z, c)).wait_recv()
        copy = rcopy(block, block, cs_sem.at[i], cr_sem.at[i], partner)
        copy.start()
        sends.append(copy)
    for i, o in enumerate(x_from + [x]):
        block = rr.at[1 - c, o]
        rcopy(block, block, cs_sem.at[i], cr_sem.at[i], partner).wait_recv()
    rcopy(a_own, afull.at[:, 1 - c], a_sem.at[0], a_sem.at[1], partner).wait_recv()

    rows = 2 * slots
    quarter = rows // ny
    tag = rr[:, :, :, 2 * width : sw].reshape(rows, 128).astype(F32)
    mask = tag > 0
    slot_prob = jnp.max(tag, axis=1, keepdims=True)
    xin = rr[:, :, :, 0:width].reshape(rows, width)
    dyin = rr[:, :, :, width : 2 * width].reshape(rows, width)
    at = afull[...].astype(F32).reshape(128, width).astype(BF)

    def y_send(index, src, dst):
        for i, o in enumerate(y_others):
            copy = ycopy(src(o), dst, ys_sem.at[index, i], yr_sem.at[index, i], o)
            copy.start()
            sends.append(copy)

    def put(index, value):
        part_f[index] = value
        part_b[index] = value.astype(BF).reshape(ny, quarter, hid)
        y_send(index, lambda o: part_b.at[index, o], yr.at[index, y])

    w_copies[0].wait()
    put(0, mm(xin, wg[...]))
    w_copies[1].wait()
    put(1, mm(xin, wu[...]))
    w_copies[2].wait()
    put(2, mm_t(dyin, wd[...]) * slot_prob)
    projected = jnp.where(mask, mm_t(xin, at), 0.0)
    proj_f[...] = projected
    proj_b[...] = projected.astype(BF).reshape(ny, quarter, 128)
    y_send(3, lambda o: proj_b.at[o], yx.at[y])

    y_back = (2, 3, 1) if ny == 4 else range(ny - 1, 0, -1)
    y_from = [lax.rem(y + d, ny) for d in y_back]
    mine = pl.ds(pl.multiple_of(y * quarter, quarter), quarter)

    def total(index):
        value = part_f[index, mine, :]
        for i, o in enumerate(y_from):
            block = yr.at[index, o]
            ycopy(block, block, ys_sem.at[index, i], yr_sem.at[index, i], o).wait_recv()
            value = value + yr[index, o].astype(F32)
        return value

    gate = total(0)
    up = total(1)
    act = total(2)
    low = proj_f[mine, :]
    for i, o in enumerate(y_from):
        block = yx.at[o]
        ycopy(block, block, ys_sem.at[3, i], yr_sem.at[3, i], o).wait_recv()
        low = low + yx[o].astype(F32)
    lane = iota((quarter, 128), 1)
    bmap = b_map[...]
    gate = gate + ADAPTER_SCALE * mm(jnp.where(lane < 64, low, 0.0).astype(BF), bmap)
    up = up + ADAPTER_SCALE * mm(jnp.where(lane < 64, 0.0, low).astype(BF), bmap)
    sig = 1.0 / (1.0 + jnp.exp(-gate))
    dgu[y, :, 0:hid] = (act * up * sig * (1.0 + gate * (1.0 - sig))).astype(BF)
    dgu[y, :, hid : 2 * hid] = (act * gate * sig).astype(BF)
    xsf[y] = low.astype(BF)
    for i, o in enumerate(y_others):
        copy = ycopy(dgu.at[y], dgu.at[y], gs_sem.at[0, i], gr_sem.at[0, i], o)
        copy.start()
        sends.append(copy)
    for i, o in enumerate(y_others):
        copy = ycopy(xsf.at[y], xsf.at[y], gs_sem.at[1, i], gr_sem.at[1, i], o)
        copy.start()
        sends.append(copy)
    for i, o in enumerate(y_from):
        block = dgu.at[o]
        ycopy(block, block, gs_sem.at[0, i], gr_sem.at[0, i], o).wait_recv()
    for i, o in enumerate(y_from):
        block = xsf.at[o]
        ycopy(block, block, gs_sem.at[1, i], gr_sem.at[1, i], o).wait_recv()

    hq = ny // 2
    wide = iota((slots, 128), 1)

    def back_half(which):
        group = pl.ds(which * hq, hq)
        dg = dgu[group, :, 0:hid].reshape(slots, hid)
        du = dgu[group, :, hid : 2 * hid].reshape(slots, hid)
        marks = rr[which, :, :, 2 * width : sw].reshape(slots, 128).astype(F32) > 0
        q = jnp.where(wide < 64, mm_t(dg, bmap), mm_t(du, bmap))
        q = jnp.where(marks, ADAPTER_SCALE * q, 0.0)
        r = mm_t(dg, wg[...]) + mm_t(du, wu[...]) + mm(q.astype(BF), at)
        qs[which] = q
        return r.reshape(nx, slots_x, width)

    rsend[...] = back_half(1 - c).astype(BF)
    order = x_others + [x]
    order_from = x_from + [x]
    for i, o in enumerate(order):
        copy = rcopy(rsend.at[o], rrecv.at[o], rc_s.at[i], rc_r.at[i], partner)
        copy.start()
        sends.append(copy)
    sb[...] = back_half(c).astype(BF)
    q_copy = rcopy(qs, qr, q_sem.at[0], q_sem.at[1], partner)
    q_copy.start()
    sends.append(q_copy)
    for i, o in enumerate(order):
        block = rrecv.at[o]
        rcopy(block, block, rc_s.at[i], rc_r.at[i], partner).wait_recv()
        both = (sb[o].astype(F32) + rrecv[o].astype(F32)).astype(BF)
        if i < nx - 1:
            sb[o] = both
            copy = rcopy(sb.at[o], xb.at[x], bx_s.at[i], bx_r.at[i], eid(o, z, c))
            copy.start()
            sends.append(copy)
        else:
            xb[o] = both

    dg = dgu[:, :, 0:hid].reshape(rows, hid)
    du = dgu[:, :, hid : 2 * hid].reshape(rows, hid)
    low_t = xsf[...].reshape(rows, 128).astype(F32).T.astype(BF)
    bg_rows = iota((128, hid), 0)
    bg_out[...] = ADAPTER_SCALE * jnp.where(bg_rows < 64, mm(low_t, dg), mm(low_t, du))

    for i, o in enumerate(x_from):
        block = xb.at[o]
        rcopy(block, block, bx_s.at[i], bx_r.at[i], eid(o, z, c)).wait_recv()
    by_token = mm(sel[...], xb[...].reshape(slots, width))
    tz[...] = by_token.reshape(nz, ntok, width).astype(BF)
    dist = []
    for d in range(far, 0, -1):
        dist.append(d)
        if d != nz - d:
            dist.append(nz - d)
    for i, d in enumerate(dist):
        o = lax.rem(z + d, nz)
        copy = rcopy(tz.at[o], fb.at[z], bz_s.at[d - 1], bz_r.at[d - 1], eid(x, o, c))
        copy.start()
        sends.append(copy)
    fb[z] = tz[z]

    q_copy.wait_recv()
    q_all = (qs[...] + qr[...]).reshape(rows, 128)
    ag = mm(q_all.T.astype(BF), xin).reshape(8, 2, 8, width)
    ag_out[...] = jnp.where(c == 0, ag[:, 0], ag[:, 1])

    for d in dist:
        o = lax.rem(z + nz - d, nz)
        block = fb.at[o]
        rcopy(block, block, bz_s.at[d - 1], bz_r.at[d - 1], eid(x, o, c)).wait_recv()
    ig_out[...] = jnp.sum(fb[...].astype(F32), axis=0).astype(BF)
    for copy in sends:
        copy.wait_send()


def shards(
    tokens,
    output_gradient,
    routes,
    router_expert_weight,
    tenant,
    gate_weight,
    up_weight,
    down_weight,
    adapter_input_maps,
    adapter_output_maps,
    nx=CHIPS_X,
):
    devices = lax.axis_size("expert")
    ny = lax.axis_size("dp")
    nz = devices // (2 * nx)
    ntok, width = tokens.shape
    hid = gate_weight.shape[2]
    slots_x = 2 * nz
    slots = nx * slots_x
    rows = 2 * slots
    quarter = rows // ny
    lm = slots
    pw = 2 * width + lm + 128
    sw = 2 * width + 128
    a_own = jnp.transpose(adapter_input_maps[0], (1, 2, 3, 0)).reshape(8, 8, width)
    b_map = adapter_output_maps.reshape(128, hid)
    vmem = pl.BlockSpec(memory_space=pltpu.VMEM)
    anywhere = pl.BlockSpec(memory_space=pl.ANY)
    dma = pltpu.SemaphoreType.DMA
    far = nz // 2
    ig, ag, bg = pl.pallas_call(
        functools.partial(kernel, nx, nz, ny),
        out_shape=(
            jax.ShapeDtypeStruct((ntok, width), BF),
            jax.ShapeDtypeStruct((8, 8, width), F32),
            jax.ShapeDtypeStruct((128, hid), F32),
        ),
        in_specs=[vmem] * 7 + [anywhere] * 3,
        out_specs=(vmem, vmem, vmem),
        scratch_shapes=[
            pltpu.VMEM((width, hid), BF),
            pltpu.VMEM((width, hid), BF),
            pltpu.VMEM((hid, width), BF),
            pltpu.VMEM((nz, ntok, pw), BF),
            pltpu.VMEM((nz * ntok, slots), BF),
            pltpu.VMEM((nx, slots_x, sw), BF),
            pltpu.VMEM((2, nx, slots_x, sw), BF),
            pltpu.VMEM((8, 2, 8, width), BF),
            pltpu.VMEM((3, rows, hid), F32),
            pltpu.VMEM((3, ny, quarter, hid), BF),
            pltpu.VMEM((rows, 128), F32),
            pltpu.VMEM((ny, quarter, 128), BF),
            pltpu.VMEM((3, ny, quarter, hid), BF),
            pltpu.VMEM((ny, quarter, 128), BF),
            pltpu.VMEM((ny, quarter, 2 * hid), BF),
            pltpu.VMEM((ny, quarter, 128), BF),
            pltpu.VMEM((2, slots, 128), F32),
            pltpu.VMEM((2, slots, 128), F32),
            pltpu.VMEM((nx, slots_x, width), BF),
            pltpu.VMEM((nx, slots_x, width), BF),
            pltpu.VMEM((nx, slots_x, width), BF),
            pltpu.VMEM((nx, slots_x, width), BF),
            pltpu.VMEM((nz, ntok, width), BF),
            pltpu.VMEM((nz, ntok, width), BF),
            dma((3,)),
            dma((2,)),
            dma((2 * far,)),
            dma((2 * far,)),
            dma((nx - 1,)),
            dma((nx - 1,)),
            dma((nx,)),
            dma((nx,)),
            dma((4, ny - 1)),
            dma((4, ny - 1)),
            dma((2, ny - 1)),
            dma((2, ny - 1)),
            dma((2,)),
            dma((nx,)),
            dma((nx,)),
            dma((nx - 1,)),
            dma((nx - 1,)),
            dma((nz - 1,)),
            dma((nz - 1,)),
        ],
        compiler_params=pltpu.CompilerParams(collective_id=0, has_side_effects=True),
        name="layer_backward",
    )(
        tokens,
        output_gradient,
        routes,
        router_expert_weight,
        tenant.reshape(ntok, 1),
        a_own,
        b_map,
        gate_weight[0],
        up_weight[0],
        down_weight[0],
    )
    adapter_a_grad = jnp.transpose(ag.reshape(2, 4, 8, width), (3, 0, 1, 2))[None]
    adapter_b_grad = bg.reshape(1, 2, 4, 16, hid)
    return (ig, adapter_a_grad, adapter_b_grad)


def solution(mesh):
    placed = (
        P("expert", "dp"),
        P("expert", "dp"),
        P("expert", None),
        P("expert", None),
        P("expert"),
        P("expert", "dp", None),
        P("expert", "dp", None),
        P("expert", None, "dp"),
        P("expert", "dp", None, None, None),
        P("expert", None, None, None, None),
    )
    return jax.shard_map(
        shards,
        mesh=mesh,
        in_specs=placed,
        out_specs=(
            P("expert", "dp"),
            P("expert", "dp", None, None, None),
            P("expert", None, None, None, None),
        ),
        check_vma=False,
    )
```

```python
import functools

import jax
import jax.numpy as jnp
from jax import lax
from jax.experimental import pallas as pl
from jax.experimental.pallas import tpu as pltpu
from jax.sharding import PartitionSpec as P

ADAPTER_SCALE = 2.0
CHIPS_X = 4
HOP = 2
GROUPS = 2
BF = jnp.bfloat16
F32 = jnp.float32
MESH = pl.DeviceIdType.MESH


def mm(a, b):
    return lax.dot_general(a, b, (((1,), (0,)), ((), ())), preferred_element_type=F32)


def mm_t(a, b):
    return lax.dot_general(a, b, (((1,), (1,)), ((), ())), preferred_element_type=F32)


def iota(shape, axis):
    return lax.broadcasted_iota(jnp.int32, shape, axis)


def kernel(
    nx,
    nz,
    ny,
    tok,
    dy,
    routes,
    prob,
    ten,
    a_own,
    b_map,
    wg_hbm,
    wu_hbm,
    wd_hbm,
    ig_out,
    ag_out,
    bg_out,
    wg,
    wu,
    wd,
    pg,
    sel,
    rs,
    rr,
    afull,
    part_f,
    part_b,
    proj_f,
    proj_b,
    yr,
    yx,
    dgu,
    xsf,
    qs,
    qr,
    rfull,
    rrecv,
    sb,
    xb,
    tz,
    fb,
    w_sem,
    a_sem,
    ring_s,
    ring_r,
    xs_sem,
    xr_sem,
    cs_sem,
    cr_sem,
    ys_sem,
    yr_sem,
    gs_sem,
    gr_sem,
    q_sem,
    rc_s,
    rc_r,
    bx_s,
    bx_r,
    bz_s,
    bz_r,
):
    me = lax.axis_index("expert")
    y = lax.axis_index("dp")
    c = lax.rem(me, 2)
    z = lax.rem(lax.div(me, 2), nz)
    x = lax.div(me, 2 * nz)
    width = tok.shape[1]
    hid = wg.shape[1]
    ntok = tok.shape[0]
    lm = 2 * nx * nz
    pw = 2 * width + lm + 128
    sw = 2 * width + 128
    far = nz // 2
    gz = nz // GROUPS
    off = gz // 2 - 1
    slots_x = 2 * gz
    slots = nx * slots_x
    rows = 2 * slots
    quarter = rows // ny
    count = gz * ntok

    def eid(xx, zz, cc):
        return (xx * nz + zz) * 2 + cc

    partner = eid(x, z, 1 - c)
    z_near = []
    for d in range(1, nz):
        z_near.append(eid(x, lax.rem(z + d, nz), c))

    def rcopy(src, dst, s_sem, r_sem, dev):
        return pltpu.make_async_remote_copy(
            src_ref=src,
            dst_ref=dst,
            send_sem=s_sem,
            recv_sem=r_sem,
            device_id={"expert": dev},
            device_id_type=MESH,
        )

    def ycopy(src, dst, s_sem, r_sem, dev):
        return pltpu.make_async_remote_copy(
            src_ref=src,
            dst_ref=dst,
            send_sem=s_sem,
            recv_sem=r_sem,
            device_id={"dp": dev},
            device_id_type=MESH,
        )

    barrier = pltpu.get_barrier_semaphore()
    x_others = [lax.rem(x + d, nx) for d in ((2, 1, 3) if nx == 4 else range(1, nx))]
    y_others = [lax.rem(y + d, ny) for d in ((2, 1, 3) if ny == 4 else range(1, ny))]
    near = z_near + [partner] + [eid(o, z, c) for o in x_others]
    for dev in near:
        pl.semaphore_signal(barrier, inc=1, device_id={"expert": dev}, device_id_type=MESH)
    for dev in y_others:
        pl.semaphore_signal(barrier, inc=1, device_id={"dp": dev}, device_id_type=MESH)

    w_copies = [
        pltpu.make_async_copy(wg_hbm, wg, w_sem.at[0]),
        pltpu.make_async_copy(wu_hbm, wu, w_sem.at[1]),
        pltpu.make_async_copy(wd_hbm, wd, w_sem.at[2]),
    ]
    for w_copy in w_copies:
        w_copy.start()

    col = iota((ntok, lm), 1)
    row = iota((ntok, lm), 0)
    col_expert = lax.div(lax.rem(col, 2 * nx), 2) * nz + lax.div(col, 2 * nx)
    col_pos = lax.rem(col, 2)
    hit = jnp.zeros((ntok, lm), jnp.int32)
    weight = jnp.zeros((ntok, lm), F32)
    chosen = routes[...]
    probs = prob[...].astype(F32)
    for k in range(routes.shape[1]):
        same = chosen[:, k : k + 1] == col_expert
        hit = hit + same.astype(jnp.int32)
        weight = weight + jnp.where(same, probs[:, k : k + 1], 0.0)
    before = jnp.zeros((ntok, lm), jnp.int32)
    for n in range(ntok - 1):
        before = before + jnp.where(row > n, hit[n : n + 1, :], 0)
    weight = jnp.where(before == col_pos, weight, 0.0)
    lane_ten = lax.rem(lax.div(iota((ntok, 128), 1), 16), 4)
    ten_hot = (ten[...] == lane_ten).astype(F32)
    pg[off, :, 0:width] = tok[...]
    pg[off, :, width : 2 * width] = dy[...]
    pg[off, :, 2 * width : 2 * width + lm] = weight.astype(BF)
    pg[off, :, 2 * width + lm : pw] = ten_hot.astype(BF)
    afull[:, c] = a_own[...]

    pl.semaphore_wait(barrier, len(near) + len(y_others))

    a_copy = rcopy(a_own, afull.at[:, c], a_sem.at[0], a_sem.at[1], partner)

    sends = []
    arrived = set()

    def place(direction, d):
        return (off - d) % nz if direction == 0 else (off + d) % nz

    def ring(direction, d):
        skip = min(d, HOP)
        dev = lax.rem(z + skip, nz) if direction == 0 else lax.rem(z + nz - skip, nz)
        at = direction * far + d - 1
        return rcopy(
            pg.at[place(direction, d - skip)],
            pg.at[place(direction, d)],
            ring_s.at[at],
            ring_r.at[at],
            eid(x, dev, c),
        )

    def need(direction, d):
        if d > 0 and (direction, d) not in arrived:
            arrived.add((direction, d))
            ring(direction, d).wait_recv()

    def send(copy):
        copy.start()
        sends.append(copy)

    def advance(first, last):
        for d in range(first, last + 1):
            for direction in range(2):
                if direction == 1 and d == far:
                    continue
                need(direction, d - HOP)
                send(ring(direction, d))

    def select(g):
        gathered = pg[g * gz : (g + 1) * gz].astype(F32).reshape(count, pw).astype(BF)
        meta = gathered[:, 2 * width : 2 * width + lm]
        tenants = gathered[:, 2 * width + lm : pw]
        j = iota((slots, lm), 0)
        pick = (
            iota((slots, lm), 1) == z * (2 * nx) + lax.div(j, slots_x) * 2 + lax.rem(j, 2)
        ).astype(BF)
        slot_z = lax.div(lax.rem(iota((slots, count), 0), slots_x), 2)
        tok_z = lax.div(iota((slots, count), 1), ntok)
        weights_t = jnp.where(slot_z == tok_z, mm_t(pick, meta), 0.0)
        select_t = (weights_t > 0).astype(BF)
        slot_z2 = lax.div(lax.rem(iota((count, slots), 1), slots_x), 2)
        tok_z2 = lax.div(iota((count, slots), 0), ntok)
        weights_n = jnp.where(slot_z2 == tok_z2, mm_t(meta, pick), 0.0)
        sel[g] = (weights_n > 0).astype(BF)
        rs[g, :, :, 0 : 2 * width] = (
            mm(select_t, gathered[:, 0 : 2 * width]).astype(BF).reshape(nx, slots_x, 2 * width)
        )
        rs[g, :, :, 2 * width : sw] = (
            mm(weights_t.astype(BF), tenants).astype(BF).reshape(nx, slots_x, 128)
        )

    back = (2, 3, 1) if nx == 4 else range(nx - 1, 0, -1)
    x_from = [lax.rem(x + d, nx) for d in back]

    def x_send(g):
        for i, o in enumerate(x_others):
            send(rcopy(rs.at[g, o], rr.at[g, c, x], xs_sem.at[g, i], xr_sem.at[g, i], eid(o, z, c)))
        last = nx - 1
        send(rcopy(rs.at[g, x], rr.at[g, c, x], cs_sem.at[g, last], cr_sem.at[g, last], partner))
        rr[g, c, x] = rs[g, x]

    def x_recv(g):
        for i, o in enumerate(x_from):
            block = rr.at[g, c, o]
            rcopy(block, block, xs_sem.at[g, i], xr_sem.at[g, i], eid(o, z, c)).wait_recv()
            send(rcopy(block, block, cs_sem.at[g, i], cr_sem.at[g, i], partner))

    def c_recv(g):
        for i, o in enumerate(x_from + [x]):
            block = rr.at[g, 1 - c, o]
            rcopy(block, block, cs_sem.at[g, i], cr_sem.at[g, i], partner).wait_recv()

    bmap = b_map[...]

    def adapters():
        return afull[...].astype(F32).reshape(128, width).astype(BF)

    def marks(g):
        return rr[g, :, :, :, 2 * width : sw].reshape(rows, 128).astype(F32)

    def y_send(g, index, src, dst):
        for i, o in enumerate(y_others):
            send(ycopy(src(o), dst, ys_sem.at[g, index, i], yr_sem.at[g, index, i], o))

    def partial(g):
        tag = marks(g)
        slot_prob = jnp.max(tag, axis=1, keepdims=True)
        xin = rr[g, :, :, :, 0:width].reshape(rows, width)
        dyin = rr[g, :, :, :, width : 2 * width].reshape(rows, width)

        def put(index, value):
            part_f[g, index] = value
            part_b[g, index] = value.astype(BF).reshape(ny, quarter, hid)
            y_send(g, index, lambda o: part_b.at[g, index, o], yr.at[g, index, y])

        if g == 0:
            w_copies[0].wait()
        put(0, mm(xin, wg[...]))
        if g == 0:
            w_copies[1].wait()
        put(1, mm(xin, wu[...]))
        if g == 0:
            w_copies[2].wait()
        put(2, mm_t(dyin, wd[...]) * slot_prob)
        projected = jnp.where(tag > 0, mm_t(xin, adapters()), 0.0)
        proj_f[g] = projected
        proj_b[g] = projected.astype(BF).reshape(ny, quarter, 128)
        y_send(g, 3, lambda o: proj_b.at[g, o], yx.at[g, y])

    y_back = (2, 3, 1) if ny == 4 else range(ny - 1, 0, -1)
    y_from = [lax.rem(y + d, ny) for d in y_back]
    mine = pl.ds(pl.multiple_of(y * quarter, quarter), quarter)

    def total(g, index):
        value = part_f[g, index, mine, :]
        for i, o in enumerate(y_from):
            block = yr.at[g, index, o]
            ycopy(block, block, ys_sem.at[g, index, i], yr_sem.at[g, index, i], o).wait_recv()
            value = value + yr[g, index, o].astype(F32)
        return value

    def act_grads(g):
        gate = total(g, 0)
        up = total(g, 1)
        act = total(g, 2)
        low = proj_f[g, mine, :]
        for i, o in enumerate(y_from):
            block = yx.at[g, o]
            ycopy(block, block, ys_sem.at[g, 3, i], yr_sem.at[g, 3, i], o).wait_recv()
            low = low + yx[g, o].astype(F32)
        lane = iota((quarter, 128), 1)
        gate = gate + ADAPTER_SCALE * mm(jnp.where(lane < 64, low, 0.0).astype(BF), bmap)
        up = up + ADAPTER_SCALE * mm(jnp.where(lane < 64, 0.0, low).astype(BF), bmap)
        sig = 1.0 / (1.0 + jnp.exp(-gate))
        dgu[g, y, :, 0:hid] = (act * up * sig * (1.0 + gate * (1.0 - sig))).astype(BF)
        dgu[g, y, :, hid : 2 * hid] = (act * gate * sig).astype(BF)
        xsf[g, y] = low.astype(BF)
        for k, ref in enumerate((dgu, xsf)):
            mine_of = ref.at[g, y]
            for i, o in enumerate(y_others):
                send(ycopy(mine_of, mine_of, gs_sem.at[g, k, i], gr_sem.at[g, k, i], o))

    def g_recv(g):
        for k, ref in enumerate((dgu, xsf)):
            for i, o in enumerate(y_from):
                block = ref.at[g, o]
                ycopy(block, block, gs_sem.at[g, k, i], gr_sem.at[g, k, i], o).wait_recv()

    order = x_others + [x]

    def back_send(g):
        dg = dgu[g, :, :, 0:hid].reshape(rows, hid)
        du = dgu[g, :, :, hid : 2 * hid].reshape(rows, hid)
        wide = iota((rows, 128), 1)
        q = jnp.where(wide < 64, mm_t(dg, bmap), mm_t(du, bmap))
        q = jnp.where(marks(g) > 0, ADAPTER_SCALE * q, 0.0)
        r = mm_t(dg, wg[...]) + mm_t(du, wu[...]) + mm(q.astype(BF), adapters())
        qs[g] = q
        rfull[g] = r.astype(BF).reshape(2, nx, slots_x, width)
        for i, o in enumerate(order):
            send(rcopy(rfull.at[g, 1 - c, o], rrecv.at[g, o], rc_s.at[g, i], rc_r.at[g, i], partner))
        send(q_copy(g))

    def q_copy(g):
        return rcopy(qs.at[g], qr.at[g], q_sem.at[g, 0], q_sem.at[g, 1], partner)

    def back_x(g):
        for i, o in enumerate(order):
            block = rrecv.at[g, o]
            rcopy(block, block, rc_s.at[g, i], rc_r.at[g, i], partner).wait_recv()
            both = (rfull[g, c, o].astype(F32) + rrecv[g, o].astype(F32)).astype(BF)
            if i < nx - 1:
                sb[g, o] = both
                send(rcopy(sb.at[g, o], xb.at[g, x], bx_s.at[g, i], bx_r.at[g, i], eid(o, z, c)))
            else:
                xb[g, o] = both

    def home(g):
        for i, o in enumerate(x_from):
            block = xb.at[g, o]
            rcopy(block, block, bx_s.at[g, i], bx_r.at[g, i], eid(o, z, c)).wait_recv()
        by_token = mm(sel[g], xb[g].reshape(slots, width))
        tz[g * gz : (g + 1) * gz] = by_token.reshape(gz, ntok, width).astype(BF)
        dist = [(q - off) % nz for q in range(g * gz, (g + 1) * gz)]
        for d in sorted(dist, key=lambda d: -min(d, nz - d)):
            q = (d + off) % nz
            if d == 0:
                fb[0] = tz[q]
                continue
            o = lax.rem(z + d, nz)
            send(rcopy(tz.at[q], fb.at[d], bz_s.at[d - 1], bz_r.at[d - 1], eid(x, o, c)))

    step = min(HOP, far)
    advance(1, step)
    send(a_copy)
    advance(step + 1, max(step, far - HOP))
    for d in range(1, off + 1):
        need(0, d)
    for d in range(1, gz - off):
        need(1, d)
    select(0)
    x_send(0)
    advance(max(step, far - HOP) + 1, far)
    x_recv(0)
    for d in range(1, far + 1):
        need(0, d)
        if d < far:
            need(1, d)
    select(1)
    x_send(1)
    rcopy(a_own, afull.at[:, 1 - c], a_sem.at[0], a_sem.at[1], partner).wait_recv()
    c_recv(0)
    partial(0)
    x_recv(1)
    act_grads(0)
    c_recv(1)
    partial(1)
    g_recv(0)
    back_send(0)
    act_grads(1)
    back_x(0)
    home(0)
    g_recv(1)
    back_send(1)
    back_x(1)

    every = GROUPS * rows
    dg = dgu[:, :, :, 0:hid].reshape(every, hid)
    du = dgu[:, :, :, hid : 2 * hid].reshape(every, hid)
    low_t = xsf[...].reshape(every, 128).astype(F32).T.astype(BF)
    bg_rows = iota((128, hid), 0)
    bg_out[...] = ADAPTER_SCALE * jnp.where(bg_rows < 64, mm(low_t, dg), mm(low_t, du))
    home(1)

    for g in range(GROUPS):
        q_copy(g).wait_recv()
    q_all = (qs[...] + qr[...]).reshape(every, 128)
    xin = rr[:, :, :, :, 0:width].reshape(every, width)
    ag = mm(q_all.T.astype(BF), xin).reshape(8, 2, 8, width)
    ag_out[...] = jnp.where(c == 0, ag[:, 0], ag[:, 1])

    for d in range(1, nz):
        o = lax.rem(z + nz - d, nz)
        block = fb.at[d]
        rcopy(block, block, bz_s.at[d - 1], bz_r.at[d - 1], eid(x, o, c)).wait_recv()
    ig_out[...] = jnp.sum(fb[...].astype(F32), axis=0).astype(BF)
    for copy in sends:
        copy.wait_send()


def shards(
    tokens,
    output_gradient,
    routes,
    router_expert_weight,
    tenant,
    gate_weight,
    up_weight,
    down_weight,
    adapter_input_maps,
    adapter_output_maps,
    nx=CHIPS_X,
):
    devices = lax.axis_size("expert")
    ny = lax.axis_size("dp")
    nz = devices // (2 * nx)
    ntok, width = tokens.shape
    hid = gate_weight.shape[2]
    slots_x = 2 * nz // GROUPS
    slots = nx * slots_x
    rows = 2 * slots
    quarter = rows // ny
    count = nz // GROUPS * ntok
    lm = 2 * nx * nz
    pw = 2 * width + lm + 128
    sw = 2 * width + 128
    a_own = jnp.transpose(adapter_input_maps[0], (1, 2, 3, 0)).reshape(8, 8, width)
    b_map = adapter_output_maps.reshape(128, hid)
    vmem = pl.BlockSpec(memory_space=pltpu.VMEM)
    anywhere = pl.BlockSpec(memory_space=pl.ANY)
    dma = pltpu.SemaphoreType.DMA
    far = nz // 2
    ig, ag, bg = pl.pallas_call(
        functools.partial(kernel, nx, nz, ny),
        out_shape=(
            jax.ShapeDtypeStruct((ntok, width), BF),
            jax.ShapeDtypeStruct((8, 8, width), F32),
            jax.ShapeDtypeStruct((128, hid), F32),
        ),
        in_specs=[vmem] * 7 + [anywhere] * 3,
        out_specs=(vmem, vmem, vmem),
        scratch_shapes=[
            pltpu.VMEM((width, hid), BF),
            pltpu.VMEM((width, hid), BF),
            pltpu.VMEM((hid, width), BF),
            pltpu.VMEM((nz, ntok, pw), BF),
            pltpu.VMEM((GROUPS, count, slots), BF),
            pltpu.VMEM((GROUPS, nx, slots_x, sw), BF),
            pltpu.VMEM((GROUPS, 2, nx, slots_x, sw), BF),
            pltpu.VMEM((8, 2, 8, width), BF),
            pltpu.VMEM((GROUPS, 3, rows, hid), F32),
            pltpu.VMEM((GROUPS, 3, ny, quarter, hid), BF),
            pltpu.VMEM((GROUPS, rows, 128), F32),
            pltpu.VMEM((GROUPS, ny, quarter, 128), BF),
            pltpu.VMEM((GROUPS, 3, ny, quarter, hid), BF),
            pltpu.VMEM((GROUPS, ny, quarter, 128), BF),
            pltpu.VMEM((GROUPS, ny, quarter, 2 * hid), BF),
            pltpu.VMEM((GROUPS, ny, quarter, 128), BF),
            pltpu.VMEM((GROUPS, rows, 128), F32),
            pltpu.VMEM((GROUPS, rows, 128), F32),
            pltpu.VMEM((GROUPS, 2, nx, slots_x, width), BF),
            pltpu.VMEM((GROUPS, nx, slots_x, width), BF),
            pltpu.VMEM((GROUPS, nx, slots_x, width), BF),
            pltpu.VMEM((GROUPS, nx, slots_x, width), BF),
            pltpu.VMEM((nz, ntok, width), BF),
            pltpu.VMEM((nz, ntok, width), BF),
            dma((3,)),
            dma((2,)),
            dma((2 * far,)),
            dma((2 * far,)),
            dma((GROUPS, nx - 1)),
            dma((GROUPS, nx - 1)),
            dma((GROUPS, nx)),
            dma((GROUPS, nx)),
            dma((GROUPS, 4, ny - 1)),
            dma((GROUPS, 4, ny - 1)),
            dma((GROUPS, 2, ny - 1)),
            dma((GROUPS, 2, ny - 1)),
            dma((GROUPS, 2)),
            dma((GROUPS, nx)),
            dma((GROUPS, nx)),
            dma((GROUPS, nx - 1)),
            dma((GROUPS, nx - 1)),
            dma((nz - 1,)),
            dma((nz - 1,)),
        ],
        compiler_params=pltpu.CompilerParams(collective_id=0, has_side_effects=True),
        name="layer_backward",
    )(
        tokens,
        output_gradient,
        routes,
        router_expert_weight,
        tenant.reshape(ntok, 1),
        a_own,
        b_map,
        gate_weight[0],
        up_weight[0],
        down_weight[0],
    )
    adapter_a_grad = jnp.transpose(ag.reshape(2, 4, 8, width), (3, 0, 1, 2))[None]
    adapter_b_grad = bg.reshape(1, 2, 4, 16, hid)
    return (ig, adapter_a_grad, adapter_b_grad)


def solution(mesh):
    placed = (
        P("expert", "dp"),
        P("expert", "dp"),
        P("expert", None),
        P("expert", None),
        P("expert"),
        P("expert", "dp", None),
        P("expert", "dp", None),
        P("expert", None, "dp"),
        P("expert", "dp", None, None, None),
        P("expert", None, None, None, None),
    )
    return jax.shard_map(
        shards,
        mesh=mesh,
        in_specs=placed,
        out_specs=(
            P("expert", "dp"),
            P("expert", "dp", None, None, None),
            P("expert", None, None, None, None),
        ),
        check_vma=False,
    )
```

```python
import functools

import jax
import jax.numpy as jnp
from jax import lax
from jax.experimental import pallas as pl
from jax.experimental.pallas import tpu as pltpu
from jax.sharding import PartitionSpec as P

ADAPTER_SCALE = 2.0
CHIPS_X = 4
HOP = 2
GROUPS = 4
BF = jnp.bfloat16
F32 = jnp.float32
MESH = pl.DeviceIdType.MESH


def mm(a, b):
    return lax.dot_general(a, b, (((1,), (0,)), ((), ())), preferred_element_type=F32)


def mm_t(a, b):
    return lax.dot_general(a, b, (((1,), (1,)), ((), ())), preferred_element_type=F32)


def iota(shape, axis):
    return lax.broadcasted_iota(jnp.int32, shape, axis)


def kernel(
    nx,
    nz,
    ny,
    tok,
    dy,
    routes,
    prob,
    ten,
    a_own,
    b_map,
    wg_hbm,
    wu_hbm,
    wd_hbm,
    ig_out,
    ag_out,
    bg_out,
    wg,
    wu,
    wd,
    pg,
    sel,
    rs,
    rr,
    afull,
    part_f,
    part_b,
    proj_f,
    proj_b,
    yr,
    yx,
    dgu,
    xsf,
    qs,
    qr,
    rfull,
    rrecv,
    sb,
    xb,
    tz,
    fb,
    w_sem,
    a_sem,
    ring_s,
    ring_r,
    xs_sem,
    xr_sem,
    cs_sem,
    cr_sem,
    ys_sem,
    yr_sem,
    gs_sem,
    gr_sem,
    q_sem,
    rc_s,
    rc_r,
    bx_s,
    bx_r,
    bz_s,
    bz_r,
):
    me = lax.axis_index("expert")
    y = lax.axis_index("dp")
    c = lax.rem(me, 2)
    z = lax.rem(lax.div(me, 2), nz)
    x = lax.div(me, 2 * nz)
    width = tok.shape[1]
    hid = wg.shape[1]
    ntok = tok.shape[0]
    lm = 2 * nx * nz
    pw = 2 * width + lm + 128
    sw = 2 * width + 128
    far = nz // 2
    gz = nz // GROUPS
    spots = [0]
    for d in range(1, far):
        spots += [d, nz - d]
    spots.append(far)
    slots_x = 2 * gz
    slots = nx * slots_x
    rows = 2 * slots
    quarter = rows // ny
    count = gz * ntok

    def eid(xx, zz, cc):
        return (xx * nz + zz) * 2 + cc

    partner = eid(x, z, 1 - c)
    z_near = []
    for d in range(1, nz):
        z_near.append(eid(x, lax.rem(z + d, nz), c))

    def rcopy(src, dst, s_sem, r_sem, dev):
        return pltpu.make_async_remote_copy(
            src_ref=src,
            dst_ref=dst,
            send_sem=s_sem,
            recv_sem=r_sem,
            device_id={"expert": dev},
            device_id_type=MESH,
        )

    def ycopy(src, dst, s_sem, r_sem, dev):
        return pltpu.make_async_remote_copy(
            src_ref=src,
            dst_ref=dst,
            send_sem=s_sem,
            recv_sem=r_sem,
            device_id={"dp": dev},
            device_id_type=MESH,
        )

    barrier = pltpu.get_barrier_semaphore()
    x_others = [lax.rem(x + d, nx) for d in ((2, 1, 3) if nx == 4 else range(1, nx))]
    y_others = [lax.rem(y + d, ny) for d in ((2, 1, 3) if ny == 4 else range(1, ny))]
    near = z_near + [partner] + [eid(o, z, c) for o in x_others]
    for dev in near:
        pl.semaphore_signal(barrier, inc=1, device_id={"expert": dev}, device_id_type=MESH)
    for dev in y_others:
        pl.semaphore_signal(barrier, inc=1, device_id={"dp": dev}, device_id_type=MESH)

    w_copies = [
        pltpu.make_async_copy(wg_hbm, wg, w_sem.at[0]),
        pltpu.make_async_copy(wu_hbm, wu, w_sem.at[1]),
        pltpu.make_async_copy(wd_hbm, wd, w_sem.at[2]),
    ]
    for w_copy in w_copies:
        w_copy.start()

    col = iota((ntok, lm), 1)
    row = iota((ntok, lm), 0)
    col_expert = lax.div(lax.rem(col, 2 * nx), 2) * nz + lax.div(col, 2 * nx)
    col_pos = lax.rem(col, 2)
    hit = jnp.zeros((ntok, lm), jnp.int32)
    weight = jnp.zeros((ntok, lm), F32)
    chosen = routes[...]
    probs = prob[...].astype(F32)
    for k in range(routes.shape[1]):
        same = chosen[:, k : k + 1] == col_expert
        hit = hit + same.astype(jnp.int32)
        weight = weight + jnp.where(same, probs[:, k : k + 1], 0.0)
    before = jnp.zeros((ntok, lm), jnp.int32)
    for n in range(ntok - 1):
        before = before + jnp.where(row > n, hit[n : n + 1, :], 0)
    weight = jnp.where(before == col_pos, weight, 0.0)
    lane_ten = lax.rem(lax.div(iota((ntok, 128), 1), 16), 4)
    ten_hot = (ten[...] == lane_ten).astype(F32)
    pg[0, :, 0:width] = tok[...]
    pg[0, :, width : 2 * width] = dy[...]
    pg[0, :, 2 * width : 2 * width + lm] = weight.astype(BF)
    pg[0, :, 2 * width + lm : pw] = ten_hot.astype(BF)
    afull[:, c] = a_own[...]

    pl.semaphore_wait(barrier, len(near) + len(y_others))

    a_copy = rcopy(a_own, afull.at[:, c], a_sem.at[0], a_sem.at[1], partner)

    sends = []
    arrived = set()

    def place(direction, d):
        return spots.index((nz - d) % nz if direction == 0 else d)

    def ring(direction, d):
        skip = min(d, HOP)
        dev = lax.rem(z + skip, nz) if direction == 0 else lax.rem(z + nz - skip, nz)
        at = direction * far + d - 1
        return rcopy(
            pg.at[place(direction, d - skip)],
            pg.at[place(direction, d)],
            ring_s.at[at],
            ring_r.at[at],
            eid(x, dev, c),
        )

    def need(direction, d):
        if d > 0 and (direction, d) not in arrived:
            arrived.add((direction, d))
            ring(direction, d).wait_recv()

    def send(copy):
        copy.start()
        sends.append(copy)

    def advance(first, last):
        for d in range(first, last + 1):
            for direction in range(2):
                if direction == 1 and d == far:
                    continue
                need(direction, d - HOP)
                send(ring(direction, d))

    def select(g):
        gathered = pg[g * gz : (g + 1) * gz].astype(F32).reshape(count, pw).astype(BF)
        meta = gathered[:, 2 * width : 2 * width + lm]
        tenants = gathered[:, 2 * width + lm : pw]
        j = iota((slots, lm), 0)
        pick = (
            iota((slots, lm), 1) == z * (2 * nx) + lax.div(j, slots_x) * 2 + lax.rem(j, 2)
        ).astype(BF)
        slot_z = lax.div(lax.rem(iota((slots, count), 0), slots_x), 2)
        tok_z = lax.div(iota((slots, count), 1), ntok)
        weights_t = jnp.where(slot_z == tok_z, mm_t(pick, meta), 0.0)
        select_t = (weights_t > 0).astype(BF)
        slot_z2 = lax.div(lax.rem(iota((count, slots), 1), slots_x), 2)
        tok_z2 = lax.div(iota((count, slots), 0), ntok)
        weights_n = jnp.where(slot_z2 == tok_z2, mm_t(meta, pick), 0.0)
        sel[g] = (weights_n > 0).astype(BF)
        rs[g, :, :, 0 : 2 * width] = (
            mm(select_t, gathered[:, 0 : 2 * width]).astype(BF).reshape(nx, slots_x, 2 * width)
        )
        rs[g, :, :, 2 * width : sw] = (
            mm(weights_t.astype(BF), tenants).astype(BF).reshape(nx, slots_x, 128)
        )

    back = (2, 3, 1) if nx == 4 else range(nx - 1, 0, -1)
    x_from = [lax.rem(x + d, nx) for d in back]

    def x_send(g):
        for i, o in enumerate(x_others):
            send(rcopy(rs.at[g, o], rr.at[g, c, x], xs_sem.at[g, i], xr_sem.at[g, i], eid(o, z, c)))
        last = nx - 1
        send(rcopy(rs.at[g, x], rr.at[g, c, x], cs_sem.at[g, last], cr_sem.at[g, last], partner))
        rr[g, c, x] = rs[g, x]

    def x_recv(g):
        for i, o in enumerate(x_from):
            block = rr.at[g, c, o]
            rcopy(block, block, xs_sem.at[g, i], xr_sem.at[g, i], eid(o, z, c)).wait_recv()
            send(rcopy(block, block, cs_sem.at[g, i], cr_sem.at[g, i], partner))

    def c_recv(g):
        for i, o in enumerate(x_from + [x]):
            block = rr.at[g, 1 - c, o]
            rcopy(block, block, cs_sem.at[g, i], cr_sem.at[g, i], partner).wait_recv()

    bmap = b_map[...]

    def adapters():
        return afull[...].astype(F32).reshape(128, width).astype(BF)

    def marks(g):
        return rr[g, :, :, :, 2 * width : sw].reshape(rows, 128).astype(F32)

    def y_send(g, index, src, dst):
        for i, o in enumerate(y_others):
            send(ycopy(src(o), dst, ys_sem.at[g, index, i], yr_sem.at[g, index, i], o))

    def partial(g):
        tag = marks(g)
        slot_prob = jnp.max(tag, axis=1, keepdims=True)
        xin = rr[g, :, :, :, 0:width].reshape(rows, width)
        dyin = rr[g, :, :, :, width : 2 * width].reshape(rows, width)

        def put(index, value):
            part_f[g, index] = value
            part_b[g, index] = value.astype(BF).reshape(ny, quarter, hid)
            y_send(g, index, lambda o: part_b.at[g, index, o], yr.at[g, index, y])

        if g == 0:
            w_copies[0].wait()
        put(0, mm(xin, wg[...]))
        if g == 0:
            w_copies[1].wait()
        put(1, mm(xin, wu[...]))
        if g == 0:
            w_copies[2].wait()
        put(2, mm_t(dyin, wd[...]) * slot_prob)
        projected = jnp.where(tag > 0, mm_t(xin, adapters()), 0.0)
        proj_f[g] = projected
        proj_b[g] = projected.astype(BF).reshape(ny, quarter, 128)
        y_send(g, 3, lambda o: proj_b.at[g, o], yx.at[g, y])

    y_back = (2, 3, 1) if ny == 4 else range(ny - 1, 0, -1)
    y_from = [lax.rem(y + d, ny) for d in y_back]
    mine = pl.ds(pl.multiple_of(y * quarter, quarter), quarter)

    def total(g, index):
        value = part_f[g, index, mine, :]
        for i, o in enumerate(y_from):
            block = yr.at[g, index, o]
            ycopy(block, block, ys_sem.at[g, index, i], yr_sem.at[g, index, i], o).wait_recv()
            value = value + yr[g, index, o].astype(F32)
        return value

    def act_grads(g):
        gate = total(g, 0)
        up = total(g, 1)
        act = total(g, 2)
        low = proj_f[g, mine, :]
        for i, o in enumerate(y_from):
            block = yx.at[g, o]
            ycopy(block, block, ys_sem.at[g, 3, i], yr_sem.at[g, 3, i], o).wait_recv()
            low = low + yx[g, o].astype(F32)
        lane = iota((quarter, 128), 1)
        gate = gate + ADAPTER_SCALE * mm(jnp.where(lane < 64, low, 0.0).astype(BF), bmap)
        up = up + ADAPTER_SCALE * mm(jnp.where(lane < 64, 0.0, low).astype(BF), bmap)
        sig = 1.0 / (1.0 + jnp.exp(-gate))
        dgu[g, y, :, 0:hid] = (act * up * sig * (1.0 + gate * (1.0 - sig))).astype(BF)
        dgu[g, y, :, hid : 2 * hid] = (act * gate * sig).astype(BF)
        xsf[g, y] = low.astype(BF)
        for k, ref in enumerate((dgu, xsf)):
            mine_of = ref.at[g, y]
            for i, o in enumerate(y_others):
                send(ycopy(mine_of, mine_of, gs_sem.at[g, k, i], gr_sem.at[g, k, i], o))

    def g_recv(g):
        for k, ref in enumerate((dgu, xsf)):
            for i, o in enumerate(y_from):
                block = ref.at[g, o]
                ycopy(block, block, gs_sem.at[g, k, i], gr_sem.at[g, k, i], o).wait_recv()

    order = x_others + [x]

    def back_send(g):
        dg = dgu[g, :, :, 0:hid].reshape(rows, hid)
        du = dgu[g, :, :, hid : 2 * hid].reshape(rows, hid)
        wide = iota((rows, 128), 1)
        q = jnp.where(wide < 64, mm_t(dg, bmap), mm_t(du, bmap))
        q = jnp.where(marks(g) > 0, ADAPTER_SCALE * q, 0.0)
        r = mm_t(dg, wg[...]) + mm_t(du, wu[...]) + mm(q.astype(BF), adapters())
        qs[g] = q
        rfull[g] = r.astype(BF).reshape(2, nx, slots_x, width)
        for i, o in enumerate(order):
            send(rcopy(rfull.at[g, 1 - c, o], rrecv.at[g, o], rc_s.at[g, i], rc_r.at[g, i], partner))
        send(q_copy(g))

    def q_copy(g):
        return rcopy(qs.at[g], qr.at[g], q_sem.at[g, 0], q_sem.at[g, 1], partner)

    def back_x(g):
        for i, o in enumerate(order):
            block = rrecv.at[g, o]
            rcopy(block, block, rc_s.at[g, i], rc_r.at[g, i], partner).wait_recv()
            both = (rfull[g, c, o].astype(F32) + rrecv[g, o].astype(F32)).astype(BF)
            if i < nx - 1:
                sb[g, o] = both
                send(rcopy(sb.at[g, o], xb.at[g, x], bx_s.at[g, i], bx_r.at[g, i], eid(o, z, c)))
            else:
                xb[g, o] = both

    def home(g):
        for i, o in enumerate(x_from):
            block = xb.at[g, o]
            rcopy(block, block, bx_s.at[g, i], bx_r.at[g, i], eid(o, z, c)).wait_recv()
        by_token = mm(sel[g], xb[g].reshape(slots, width))
        tz[g * gz : (g + 1) * gz] = by_token.reshape(gz, ntok, width).astype(BF)
        dist = spots[g * gz : (g + 1) * gz]
        for d in sorted(dist, key=lambda d: -min(d, nz - d)):
            q = spots.index(d)
            if d == 0:
                fb[0] = tz[q]
                continue
            o = lax.rem(z + d, nz)
            send(rcopy(tz.at[q], fb.at[d], bz_s.at[d - 1], bz_r.at[d - 1], eid(x, o, c)))

    jumps = [(d, min(d + HOP - 1, far)) for d in range(1, far + 1, HOP)]

    def start(g):
        while jumps and len(jumps) > most_left(g):
            advance(*jumps.pop(0))
        for d in spots[g * gz : (g + 1) * gz]:
            if d >= far:
                need(0, nz - d)
            else:
                need(1, d)
        select(g)
        x_send(g)

    def most_left(g):
        return max(0, total_jumps - 1 - (g + 1) * total_jumps // GROUPS)

    def products(g):
        if g == 0:
            rcopy(a_own, afull.at[:, 1 - c], a_sem.at[0], a_sem.at[1], partner).wait_recv()
        c_recv(g)
        partial(g)

    def backward(g):
        g_recv(g)
        back_send(g)

    total_jumps = len(jumps)
    advance(*jumps.pop(0))
    send(a_copy)
    stages = [start, x_recv, products, act_grads, backward, back_x, home]
    for tick in range(GROUPS + len(stages) - 2):
        groups = [g for g in range(GROUPS) if 0 <= tick - g < len(stages)]
        for g in groups if tick < GROUPS else groups[::-1]:
            stages[tick - g](g)

    every = GROUPS * rows
    dg = dgu[:, :, :, 0:hid].reshape(every, hid)
    du = dgu[:, :, :, hid : 2 * hid].reshape(every, hid)
    low_t = xsf[...].reshape(every, 128).astype(F32).T.astype(BF)
    bg_rows = iota((128, hid), 0)
    bg_out[...] = ADAPTER_SCALE * jnp.where(bg_rows < 64, mm(low_t, dg), mm(low_t, du))
    home(GROUPS - 1)

    for g in range(GROUPS):
        q_copy(g).wait_recv()
    q_all = (qs[...] + qr[...]).reshape(every, 128)
    xin = rr[:, :, :, :, 0:width].reshape(every, width)
    ag = mm(q_all.T.astype(BF), xin).reshape(8, 2, 8, width)
    ag_out[...] = jnp.where(c == 0, ag[:, 0], ag[:, 1])

    for d in range(1, nz):
        o = lax.rem(z + nz - d, nz)
        block = fb.at[d]
        rcopy(block, block, bz_s.at[d - 1], bz_r.at[d - 1], eid(x, o, c)).wait_recv()
    ig_out[...] = jnp.sum(fb[...].astype(F32), axis=0).astype(BF)
    for copy in sends:
        copy.wait_send()


def shards(
    tokens,
    output_gradient,
    routes,
    router_expert_weight,
    tenant,
    gate_weight,
    up_weight,
    down_weight,
    adapter_input_maps,
    adapter_output_maps,
    nx=CHIPS_X,
):
    devices = lax.axis_size("expert")
    ny = lax.axis_size("dp")
    nz = devices // (2 * nx)
    ntok, width = tokens.shape
    hid = gate_weight.shape[2]
    slots_x = 2 * nz // GROUPS
    slots = nx * slots_x
    rows = 2 * slots
    quarter = rows // ny
    count = nz // GROUPS * ntok
    lm = 2 * nx * nz
    pw = 2 * width + lm + 128
    sw = 2 * width + 128
    a_own = jnp.transpose(adapter_input_maps[0], (1, 2, 3, 0)).reshape(8, 8, width)
    b_map = adapter_output_maps.reshape(128, hid)
    vmem = pl.BlockSpec(memory_space=pltpu.VMEM)
    anywhere = pl.BlockSpec(memory_space=pl.ANY)
    dma = pltpu.SemaphoreType.DMA
    far = nz // 2
    ig, ag, bg = pl.pallas_call(
        functools.partial(kernel, nx, nz, ny),
        out_shape=(
            jax.ShapeDtypeStruct((ntok, width), BF),
            jax.ShapeDtypeStruct((8, 8, width), F32),
            jax.ShapeDtypeStruct((128, hid), F32),
        ),
        in_specs=[vmem] * 7 + [anywhere] * 3,
        out_specs=(vmem, vmem, vmem),
        scratch_shapes=[
            pltpu.VMEM((width, hid), BF),
            pltpu.VMEM((width, hid), BF),
            pltpu.VMEM((hid, width), BF),
            pltpu.VMEM((nz, ntok, pw), BF),
            pltpu.VMEM((GROUPS, count, slots), BF),
            pltpu.VMEM((GROUPS, nx, slots_x, sw), BF),
            pltpu.VMEM((GROUPS, 2, nx, slots_x, sw), BF),
            pltpu.VMEM((8, 2, 8, width), BF),
            pltpu.VMEM((GROUPS, 3, rows, hid), F32),
            pltpu.VMEM((GROUPS, 3, ny, quarter, hid), BF),
            pltpu.VMEM((GROUPS, rows, 128), F32),
            pltpu.VMEM((GROUPS, ny, quarter, 128), BF),
            pltpu.VMEM((GROUPS, 3, ny, quarter, hid), BF),
            pltpu.VMEM((GROUPS, ny, quarter, 128), BF),
            pltpu.VMEM((GROUPS, ny, quarter, 2 * hid), BF),
            pltpu.VMEM((GROUPS, ny, quarter, 128), BF),
            pltpu.VMEM((GROUPS, rows, 128), F32),
            pltpu.VMEM((GROUPS, rows, 128), F32),
            pltpu.VMEM((GROUPS, 2, nx, slots_x, width), BF),
            pltpu.VMEM((GROUPS, nx, slots_x, width), BF),
            pltpu.VMEM((GROUPS, nx, slots_x, width), BF),
            pltpu.VMEM((GROUPS, nx, slots_x, width), BF),
            pltpu.VMEM((nz, ntok, width), BF),
            pltpu.VMEM((nz, ntok, width), BF),
            dma((3,)),
            dma((2,)),
            dma((2 * far,)),
            dma((2 * far,)),
            dma((GROUPS, nx - 1)),
            dma((GROUPS, nx - 1)),
            dma((GROUPS, nx)),
            dma((GROUPS, nx)),
            dma((GROUPS, 4, ny - 1)),
            dma((GROUPS, 4, ny - 1)),
            dma((GROUPS, 2, ny - 1)),
            dma((GROUPS, 2, ny - 1)),
            dma((GROUPS, 2)),
            dma((GROUPS, nx)),
            dma((GROUPS, nx)),
            dma((GROUPS, nx - 1)),
            dma((GROUPS, nx - 1)),
            dma((nz - 1,)),
            dma((nz - 1,)),
        ],
        compiler_params=pltpu.CompilerParams(collective_id=0, has_side_effects=True),
        name="layer_backward",
    )(
        tokens,
        output_gradient,
        routes,
        router_expert_weight,
        tenant.reshape(ntok, 1),
        a_own,
        b_map,
        gate_weight[0],
        up_weight[0],
        down_weight[0],
    )
    adapter_a_grad = jnp.transpose(ag.reshape(2, 4, 8, width), (3, 0, 1, 2))[None]
    adapter_b_grad = bg.reshape(1, 2, 4, 16, hid)
    return (ig, adapter_a_grad, adapter_b_grad)


def solution(mesh):
    placed = (
        P("expert", "dp"),
        P("expert", "dp"),
        P("expert", None),
        P("expert", None),
        P("expert"),
        P("expert", "dp", None),
        P("expert", "dp", None),
        P("expert", None, "dp"),
        P("expert", "dp", None, None, None),
        P("expert", None, None, None, None),
    )
    return jax.shard_map(
        shards,
        mesh=mesh,
        in_specs=placed,
        out_specs=(
            P("expert", "dp"),
            P("expert", "dp", None, None, None),
            P("expert", None, None, None, None),
        ),
        check_vma=False,
    )
```
